512 devices in a mesh: req: 64 (over z, y), tp: 8 (over x, core).
Axes of the slice: x: 4, y: 4, z: 16, core: 2. Of those that a mesh axis runs over, the one named last changes fastest.
Arguments:
- hidden_in: bfloat16 [1024, 2048], P('req'), may hold values from -6 to 6
- query: bfloat16 [1024, 2048], P('req', 'tp'), may hold values from -200 to 200
- new_kv: bfloat16 [1024, 4096], P('req', 'tp'), may hold values from -6 to 6
- pool_cache: bfloat16 [5120, 32, 4096], P('req', None, 'tp'), may hold values from -7 to 7
- prompt_table: int32 [128, 24], P('req'), may hold values from 0 to 79, as said below
- prompt_len: int32 [128], P('req'), may hold values from 32 to 768
- req_group: int32 [1024], P('req'), may hold values from 0 to 1, as said below
- cont_table: int32 [1024, 2], P('req'), may hold values from 0 to 79, as said below
- cont_len: int32 [1024], P('req'), may hold values from 1 to 63
- migration: int32 [384, 2], P('req'), may hold values from 0 to 15, as said below
- diff_lambda: float32 [8], P('tp'), may hold values from 0.2 to 0.8
- out_weight: bfloat16 [2048, 2048], P('tp'), may hold values from -0.125 to 0.125
- norm_gain: float32 [2048], replicated, may hold values from 0.1 to 1.9
Outputs:
- hidden_out: bfloat16 [1024, 2048], P('req')
- normed_out: bfloat16 [1024, 2048], P('req')
- arrived: bfloat16 [512, 64, 4096], P('req', None, 'tp')
The draws below stay inside these ranges and needn't reach their ends.
Inputs may be any that keep to these rules, and one draw needn't show every extreme that they name: `prompt_table`: entries are pages local to the row's index of req; with cont_table, each of a device's 80 pages appears exactly once. `cont_table`: local pages, each page of a device once together with prompt_table. `req_group`: A group index local to the device; every group of a device has a request. `migration`: each device lists 6 rows: a distinct local request slot and a destination offset 1 to 4 along req (with wrap); at most 2 rows of a device share an offset, and that many is reached.
All inputs are finite; a program needn't handle non-finite values.
Results may differ from the reference program's by a relative error of at most 0.012.
Values may be sent and summed in bfloat16 or wider, within the bound.
A program may use at most 64 MiB of HBM per device.

```python
import jax
import jax.numpy as jnp
from jax import lax

D = 2048
HEADS = 8
HD = 128
VD = 256
REQ_DEV = 16
GROUP_DEV = 2
PAGE = 32
PROMPT_PAGES = 24
CONT_PAGES = 2
MIG_DEV = 6
MIG_REACH = 4
MIG_CAP = 2
POOL = 80
REQS = 1024
GROUPS = 128
N_REQ = 64


def layout_tables(key):
    device_keys = jax.random.split(jax.random.fold_in(key, 11), N_REQ)
    page_perm = jax.vmap(lambda device_key: jax.random.permutation(device_key, POOL))(device_keys).astype(jnp.int32)
    prompt_table = page_perm[:, :GROUP_DEV * PROMPT_PAGES].reshape(GROUPS, PROMPT_PAGES)
    cont_table = page_perm[:, GROUP_DEV * PROMPT_PAGES:].reshape(REQS, CONT_PAGES)
    return (prompt_table, cont_table)


def draw_prompt_table(key, part):
    return layout_tables(key)[0]


def draw_cont_table(key, part):
    return layout_tables(key)[1]


def draw_prompt_len(key, part):
    lengths = jax.random.randint(jax.random.fold_in(key, 12), (GROUPS,), PAGE, PROMPT_PAGES * PAGE + 1, dtype=jnp.int32)
    longest = jax.random.randint(jax.random.fold_in(key, 13), (), 0, GROUPS, dtype=jnp.int32)
    return lengths.at[longest].set(PROMPT_PAGES * PAGE)


def draw_cont_len(key, part):
    lengths = jax.random.randint(jax.random.fold_in(key, 14), (REQS,), 1, CONT_PAGES * PAGE, dtype=jnp.int32)
    longest = jax.random.randint(jax.random.fold_in(key, 15), (), 0, REQS, dtype=jnp.int32)
    return lengths.at[longest].set(CONT_PAGES * PAGE - 1)


def draw_req_group(key, part):
    device_keys = jax.random.split(jax.random.fold_in(key, 16), N_REQ)

    def one_device(device_key):
        first_key, second_key = jax.random.split(device_key)
        labels = jnp.concatenate([jnp.arange(GROUP_DEV, dtype=jnp.int32), jax.random.randint(first_key, (REQ_DEV - GROUP_DEV,), 0, GROUP_DEV, dtype=jnp.int32)])
        return jax.random.permutation(second_key, labels)
    return jax.vmap(one_device)(device_keys).reshape(REQS)


def draw_migration(key, part):
    device_keys = jax.random.split(jax.random.fold_in(key, 17), N_REQ)

    def one_device(device_key):
        first_key, second_key = jax.random.split(device_key)
        slots = jax.random.permutation(first_key, REQ_DEV)[:MIG_DEV].astype(jnp.int32)
        offsets = (jax.random.permutation(second_key, MIG_REACH * MIG_CAP)[:MIG_DEV] // MIG_CAP + 1).astype(jnp.int32)
        return jnp.stack([slots, offsets], axis=-1)
    return jax.vmap(one_device)(device_keys).reshape(N_REQ * MIG_DEV, 2)


def anchor_keys(key):
    return jax.random.truncated_normal(jax.random.fold_in(key, 41), -6.0, 6.0, (N_REQ, HEADS * (2 * HD + VD)), jnp.float32)


def anchor_pages(key):
    prompt_table = layout_tables(key)[0]
    return prompt_table.reshape(N_REQ, GROUP_DEV, PROMPT_PAGES)[:, 0, 0] + jnp.arange(N_REQ, dtype=jnp.int32) * POOL


def draw_pool_cache(key, part):
    base = jax.random.truncated_normal(jax.random.fold_in(key, 21), -6.0, 6.0, (N_REQ * POOL, PAGE, HEADS * (2 * HD + VD)), jnp.float32)
    anchors = anchor_keys(key)
    where_page = anchor_pages(key)
    base = base.at[where_page, 0].set(anchors)
    return base.astype(jnp.bfloat16)


def draw_query(key, part):
    base = jax.random.truncated_normal(jax.random.fold_in(key, 31), -6.0, 6.0, (REQS, HEADS * 2 * HD), jnp.float32)
    return base.astype(jnp.bfloat16)


def block_levels(rng, shape, shards, least, top_value):
    def one(dim, shards_of):
        heights = jax.random.uniform(jax.random.fold_in(jax.random.fold_in(rng, 6), dim), (shards_of,), jnp.float32, least / len(shards), top_value / len(shards))
        return jnp.repeat(jnp.exp(heights), shape[dim] // shards_of).reshape((-1,) + (1,) * (len(shape) - dim - 1))

    gain = one(*shards[0])
    for cut in shards[1:]:
        gain = gain * one(*cut)
    return gain


def bell_draw(rng, dims, spread, most, pieces=(), held_as=jnp.bfloat16):
    array = jax.random.normal(rng, dims, jnp.float32) * spread
    if len(pieces) > 0:
        array = block_levels(rng, dims, pieces, -0.22, 0.18) * array
    return jnp.clip(array, min=-most, max=most).astype(held_as)


def setup_inputs(seed: int = 0) -> dict:
    arg_keys = jax.random.split(jax.random.key(seed), 14)
    return {
        "hidden_in": bell_draw(arg_keys[0], (REQS, D), 1.0, 6.0, ((0, 64),)),
        "query": draw_query(jax.random.fold_in(arg_keys[13], 71), 0),
        "new_kv": bell_draw(arg_keys[2], (REQS, HEADS * (2 * HD + VD)), 1.0, 6.0, ((0, 64), (1, 8))),
        "pool_cache": draw_pool_cache(jax.random.fold_in(arg_keys[13], 71), 0),
        "prompt_table": draw_prompt_table(jax.random.fold_in(arg_keys[13], 71), 0),
        "prompt_len": draw_prompt_len(jax.random.fold_in(arg_keys[13], 71), 0),
        "req_group": draw_req_group(jax.random.fold_in(arg_keys[13], 71), 0),
        "cont_table": draw_cont_table(jax.random.fold_in(arg_keys[13], 71), 0),
        "cont_len": draw_cont_len(jax.random.fold_in(arg_keys[13], 71), 0),
        "migration": draw_migration(jax.random.fold_in(arg_keys[13], 71), 0),
        "diff_lambda": jnp.clip(0.2 + 0.6 * jax.random.uniform(arg_keys[10], (HEADS,), jnp.float32) ** block_levels(arg_keys[10], (HEADS,), ((0, 8),), -0.2, 0.2), 0.2, 0.8),
        "out_weight": bell_draw(arg_keys[11], (HEADS * VD, D), (HEADS * VD) ** -0.5, 0.125, ((0, 8),)),
        "norm_gain": jnp.clip(1.0 + 0.18 * jax.random.normal(arg_keys[12], (D,), jnp.float32), 0.1, 1.9),
    }


def head_attention(queries, new_rows, page_pool, prompt_table, prompt_len, req_group, cont_table, cont_len, diff_lambda):
    row_count = queries.shape[0]
    head_count = diff_lambda.shape[0]
    head_width = page_pool.shape[-1] // head_count
    key_width = queries.shape[-1] // head_count // 2
    value_width = head_width - 2 * key_width
    page_len = page_pool.shape[1]
    group_count = prompt_table.shape[0]
    page_of = jnp.take_along_axis(cont_table, (cont_len // page_len)[:, None].astype(jnp.int32), axis=1)[:, 0]
    page_pool = page_pool.at[page_of, cont_len % page_len].set(new_rows)
    prompt_keys = page_pool[prompt_table].reshape(group_count, -1, head_count, head_width).astype(jnp.float32)
    cont_keys = page_pool[cont_table].reshape(row_count, -1, head_count, head_width).astype(jnp.float32)
    split_query = queries.reshape(row_count, head_count, 2, key_width).astype(jnp.float32)
    prompt_pos = jnp.arange(prompt_keys.shape[1], dtype=jnp.int32)
    cont_pos = jnp.arange(cont_keys.shape[1], dtype=jnp.int32)
    group_ids = jnp.arange(group_count, dtype=jnp.int32)
    prompt_mask = (req_group[:, None, None] == group_ids[None, :, None]) & (prompt_pos[None, None, :] < prompt_len[None, :, None])
    prompt_mask = prompt_mask[:, None]
    cont_mask = (cont_pos[None, :] <= cont_len[:, None])[:, None]
    score_scale = key_width ** (-0.5)
    prompt_values = prompt_keys[..., 2 * key_width:]
    cont_values = cont_keys[..., 2 * key_width:]
    outputs = []
    for twin_map in range(2):
        start_col = twin_map * key_width
        prompt_score = jnp.einsum('rhd,gjhd->rhgj', split_query[:, :, twin_map], prompt_keys[..., start_col:start_col + key_width]) * score_scale
        cont_score = jnp.einsum('rhd,rjhd->rhj', split_query[:, :, twin_map], cont_keys[..., start_col:start_col + key_width]) * score_scale
        prompt_score = jnp.where(prompt_mask, prompt_score, -1e+30)
        cont_score = jnp.where(cont_mask, cont_score, -1e+30)
        top_score = jnp.maximum(prompt_score.max(axis=(2, 3)), cont_score.max(axis=2))
        prompt_exp = jnp.exp(prompt_score - top_score[:, :, None, None])
        cont_exp = jnp.exp(cont_score - top_score[:, :, None])
        denominator = prompt_exp.sum(axis=(2, 3)) + cont_exp.sum(axis=2)
        prompt_weight = (prompt_exp / denominator[:, :, None, None]).astype(jnp.bfloat16).astype(jnp.float32)
        cont_weight = (cont_exp / denominator[:, :, None]).astype(jnp.bfloat16).astype(jnp.float32)
        mixture = jnp.einsum('rhgj,gjhe->rhe', prompt_weight, prompt_values) + jnp.einsum('rhj,rjhe->rhe', cont_weight, cont_values)
        outputs.append(mixture)
    difference = outputs[0] - diff_lambda[None, :, None] * outputs[1]
    normed = difference * lax.rsqrt(lax.optimization_barrier(jnp.mean(difference * difference, axis=-1, keepdims=True)) + 1e-05) * 0.8
    return (normed.astype(jnp.bfloat16).reshape(row_count, head_count * value_width), page_pool)

def send_buffer(page_pool, cont_table, cont_len, migration, reach, capacity):
    mig_slot = migration[:, 0]
    mig_off = migration[:, 1]
    entry_count = migration.shape[0]
    entry_order = jnp.arange(entry_count, dtype=jnp.int32)
    earlier = (mig_off[None, :] == mig_off[:, None]) & (entry_order[None, :] < entry_order[:, None])
    slot_place = (mig_off - 1) * capacity + lax.optimization_barrier(jnp.sum(earlier.astype(jnp.int32), axis=1)).astype(jnp.int32)
    page_rows = page_pool[cont_table[mig_slot]]
    page_rows = page_rows.reshape(entry_count, -1, page_pool.shape[-1])
    live_mask = jnp.arange(page_rows.shape[1], dtype=jnp.int32)[None, :] <= cont_len[mig_slot][:, None]
    page_rows = jnp.where(live_mask[:, :, None], page_rows, jnp.zeros_like(page_rows))
    buffer = jnp.zeros((reach * capacity,) + page_rows.shape[1:], page_rows.dtype).at[slot_place].set(page_rows)
    return buffer.reshape(reach, capacity, page_rows.shape[1], page_rows.shape[2])

def reference(hidden_in, query, new_kv, pool_cache, prompt_table, prompt_len, req_group, cont_table, cont_len, migration, diff_lambda, out_weight, norm_gain):

    def one_device(device_parts):
        query_dev, new_dev, pool_dev, prompt_dev, plen_dev, group_dev, cont_dev, clen_dev, mig_dev = device_parts
        attention, pool_new = head_attention(query_dev, new_dev, pool_dev, prompt_dev, plen_dev, group_dev, cont_dev, clen_dev, diff_lambda)
        return (attention, send_buffer(pool_new, cont_dev, clen_dev, mig_dev, MIG_REACH, MIG_CAP))
    stacked = (query.reshape(N_REQ, REQ_DEV, -1), new_kv.reshape(N_REQ, REQ_DEV, -1), pool_cache.reshape(N_REQ, POOL, PAGE, -1), prompt_table.reshape(N_REQ, GROUP_DEV, -1), prompt_len.reshape(N_REQ, GROUP_DEV), req_group.reshape(N_REQ, REQ_DEV), cont_table.reshape(N_REQ, REQ_DEV, -1), cont_len.reshape(N_REQ, REQ_DEV), migration.reshape(N_REQ, MIG_DEV, 2))
    attention, send_all = lax.map(one_device, stacked)
    attention = attention.reshape(REQS, -1)
    projected = jnp.dot(attention, out_weight, preferred_element_type=jnp.float32)
    summed = hidden_in.astype(jnp.float32) + projected
    normed = summed * lax.rsqrt(lax.optimization_barrier(jnp.mean(summed * summed, axis=-1, keepdims=True)) + 1e-05) * norm_gain
    arrived = jnp.stack([jnp.roll(send_all[:, offset - 1], offset, axis=0) for offset in range(1, MIG_REACH + 1)], axis=1)
    arrived = arrived.reshape(N_REQ * MIG_REACH * MIG_CAP, CONT_PAGES * PAGE, -1)
    return (summed.astype(jnp.bfloat16), normed.astype(jnp.bfloat16), arrived)
```

```python
import functools

import jax
import jax.numpy as jnp
from jax import lax
from jax.experimental import pallas as pl
from jax.experimental.pallas import tpu as pltpu
from jax.sharding import PartitionSpec as P

MIG_REACH = 4
MIG_CAP = 2
POOL_CHUNKS = 5
MESH = pl.DeviceIdType.MESH
F32 = jnp.float32
BF16 = jnp.bfloat16
NEG = -1e30


def layer_kernel(
    n_req,
    n_tp,
    prompt_table,
    prompt_len,
    req_group,
    cont_table,
    cont_len,
    migration,
    diff_lambda,
    hidden_in,
    query,
    new_kv,
    norm_gain,
    pool_hbm,
    weight_hbm,
    hidden_out,
    normed_out,
    arrived,
    pool,
    weight,
    new_rows,
    outgoing,
    part,
    sum_in,
    total,
    pool_sem,
    weight_sem,
    mig_send,
    mig_recv,
    sum_send,
    sum_recv,
    all_send,
    all_recv,
):
    rows, key_width = query.shape[0], query.shape[1] // 2
    pages, page_len, width = pool.shape
    value_col = 2 * key_width
    groups, group_pages = prompt_table.shape
    cont_pages = cont_table.shape[0]
    moves = migration.shape[1]
    block = total.shape[2]
    my_req = lax.axis_index("req")
    my_tp = lax.axis_index("tp")

    per_chunk = pages // POOL_CHUNKS
    pool_copies = []
    for chunk in range(POOL_CHUNKS):
        piece = pl.ds(chunk * per_chunk, per_chunk)
        pool_copies.append(
            pltpu.make_async_copy(pool_hbm.at[piece], pool.at[piece], pool_sem.at[chunk])
        )
        pool_copies[-1].start()
    weight_copy = pltpu.make_async_copy(weight_hbm, weight, weight_sem)
    weight_copy.start()

    barrier = pltpu.get_barrier_semaphore()
    for offset in range(1, MIG_REACH + 1):
        for other in (my_req + offset, my_req + n_req - offset):
            pl.semaphore_signal(
                barrier, inc=1, device_id={"req": lax.rem(other, n_req)}, device_id_type=MESH
            )
    for step in range(1, n_tp):
        pl.semaphore_signal(
            barrier, inc=1, device_id={"tp": lax.rem(my_tp + step, n_tp)}, device_id_type=MESH
        )

    new_rows[...] = new_kv[...].astype(F32)
    slot_of = []
    for move in range(moves):
        rank = jnp.int32(0)
        for earlier in range(move):
            rank = rank + (migration[1, earlier] == migration[1, move]).astype(jnp.int32)
        slot_of.append((migration[1, move] - 1) * MIG_CAP + rank)
    page_pos = lax.broadcasted_iota(jnp.int32, (page_len, width), 0)

    for copy in pool_copies:
        copy.wait()

    mig_copies = []
    for offset in range(1, MIG_REACH + 1):
        for place in range(MIG_CAP):
            slot = (offset - 1) * MIG_CAP + place
            request, present = jnp.int32(0), jnp.int32(0)
            for move in range(moves):
                here = slot_of[move] == slot
                request = jnp.where(here, migration[0, move], request)
                present = jnp.where(here, 1, present)
            length = jnp.where(present == 1, cont_len[request], -1)
            new_row = new_rows[pl.ds(request, 1), :]
            for page in range(cont_pages):
                held = pool[cont_table[page, request]].astype(F32)
                pos = page_pos + page * page_len
                kept = jnp.where(pos < length, held, 0.0)
                kept = jnp.where(pos == length, new_row, kept)
                outgoing[slot, page * page_len : (page + 1) * page_len, :] = kept.astype(BF16)
        span = pl.ds((offset - 1) * MIG_CAP, MIG_CAP)
        mig_copies.append(
            pltpu.make_async_remote_copy(
                src_ref=outgoing.at[span],
                dst_ref=arrived.at[span],
                send_sem=mig_send.at[offset - 1],
                recv_sem=mig_recv.at[offset - 1],
                device_id={"req": lax.rem(my_req + offset, n_req)},
                device_id_type=MESH,
            )
        )
    pl.semaphore_wait(barrier, 2 * MIG_REACH + n_tp - 1)
    for copy in reversed(mig_copies):
        copy.start()

    tile_pages = 8
    tile = tile_pages * page_len
    group_tiles = group_pages // tile_pages
    cont_rows = tile_pages // cont_pages
    row = lax.broadcasted_iota(jnp.int32, (rows, tile), 0)
    lane = lax.broadcasted_iota(jnp.int32, (rows, tile), 1)
    group_row = jnp.zeros((rows, tile), jnp.int32)
    length_row = jnp.zeros((rows, tile), jnp.int32)
    for request in range(rows):
        group_row = jnp.where(row == request, req_group[request], group_row)
        length_row = jnp.where(row == request, cont_len[request], length_row)

    tiles = []
    for group in range(groups):
        limit = jnp.where(group_row == group, prompt_len[group], 0)
        for part_of in range(group_tiles):
            names = [prompt_table[group, part_of * tile_pages + j] for j in range(tile_pages)]
            tiles.append((names, lane + part_of * tile < limit))
    cont_span = cont_pages * page_len
    for first in range(0, rows, cont_rows):
        names = [
            cont_table[j % cont_pages, first + j // cont_pages] for j in range(tile_pages)
        ]
        start = (row - first) * cont_span
        tiles.append((names, (lane >= start) & (lane < start + length_row)))

    scale = key_width ** (-0.5)
    queries = [query[:, twin * key_width : (twin + 1) * key_width] for twin in range(2)]
    contract_last = (((1,), (1,)), ((), ()))

    def scores(keys, mask, twin):
        product = lax.dot_general(
            queries[twin], keys, contract_last, preferred_element_type=F32
        )
        return jnp.where(mask, product * scale, NEG)

    score_tiles = []
    for names, mask in tiles:
        pair = []
        for twin in range(2):
            cols = slice(twin * key_width, (twin + 1) * key_width)
            keys = jnp.concatenate([pool[name, :, cols] for name in names], axis=0)
            pair.append(scores(keys, mask, twin))
        score_tiles.append(jnp.concatenate(pair, axis=0))
    own = lax.broadcasted_iota(jnp.int32, (rows, rows), 0) == lax.broadcasted_iota(
        jnp.int32, (rows, rows), 1
    )
    new_score = jnp.concatenate(
        [
            scores(new_kv[:, twin * key_width : (twin + 1) * key_width], own, twin)
            for twin in range(2)
        ],
        axis=0,
    )
    peak = functools.reduce(jnp.maximum, score_tiles)
    top = jnp.maximum(
        jnp.max(peak, axis=1, keepdims=True), jnp.max(new_score, axis=1, keepdims=True)
    )
    exp_tiles = [jnp.exp(score - top) for score in score_tiles]
    new_exp = jnp.exp(new_score - top)
    denominator = jnp.sum(sum(exp_tiles), axis=1, keepdims=True) + jnp.sum(
        new_exp, axis=1, keepdims=True
    )
    inverse = 1.0 / denominator
    mixture = jnp.dot(
        (new_exp * inverse).astype(BF16), new_kv[:, value_col:], preferred_element_type=F32
    )
    for (names, _), exp_tile in zip(tiles, exp_tiles):
        values = jnp.concatenate([pool[name, :, value_col:] for name in names], axis=0)
        mixture = mixture + jnp.dot(
            (exp_tile * inverse).astype(BF16), values, preferred_element_type=F32
        )
    difference = mixture[:rows] - diff_lambda[0] * mixture[rows:]
    square = jnp.mean(difference * difference, axis=1, keepdims=True)
    attention = (difference * lax.rsqrt(square + 1e-05) * 0.8).astype(BF16)

    weight_copy.wait()

    def columns(index):
        return pl.ds(pl.multiple_of(index * block, block), block)

    sum_copies = []
    for step in (4, 3, 5, 2, 6, 1, 7):
        peer = lax.rem(my_tp + step, n_tp)
        part[step] = jnp.dot(
            attention, weight[:, columns(peer)], preferred_element_type=F32
        ).astype(BF16)
        copy = pltpu.make_async_remote_copy(
            src_ref=part.at[step],
            dst_ref=sum_in.at[step],
            send_sem=sum_send.at[step],
            recv_sem=sum_recv.at[step],
            device_id={"tp": peer},
            device_id_type=MESH,
        )
        copy.start()
        sum_copies.append((step, copy))
    own_part = jnp.dot(
        attention, weight[:, columns(my_tp)], preferred_element_type=F32
    )
    summed = hidden_in[:, columns(my_tp)].astype(F32) + own_part
    for step, copy in reversed(sum_copies):
        copy.wait_recv()
        summed = summed + sum_in[step].astype(F32)
    total[my_tp] = summed.astype(BF16)
    all_copies = []
    for step in (4, 3, 5, 2, 6, 1, 7):
        peer = lax.rem(my_tp + step, n_tp)
        copy = pltpu.make_async_remote_copy(
            src_ref=total.at[my_tp],
            dst_ref=total.at[my_tp],
            send_sem=all_send.at[step],
            recv_sem=all_recv.at[step],
            device_id={"tp": peer},
            device_id_type=MESH,
        )
        copy.start()
        all_copies.append(copy)
    for copy in reversed(all_copies):
        copy.wait_recv()
    blocks = [total[index].astype(F32) for index in range(n_tp)]
    square_sum = functools.reduce(jnp.add, [value * value for value in blocks])
    mean = jnp.sum(square_sum, axis=1, keepdims=True) / (block * n_tp)
    factor = lax.rsqrt(mean + 1e-05)
    for index, value in enumerate(blocks):
        cols = slice(index * block, (index + 1) * block)
        hidden_out[:, cols] = value.astype(BF16)
        normed_out[:, cols] = (value * factor * norm_gain[:, cols]).astype(BF16)
    for _, copy in sum_copies:
        copy.wait_send()
    for copy in all_copies:
        copy.wait_send()
    for copy in mig_copies:
        copy.wait()


def shards(
    n_req,
    n_tp,
    hidden_in,
    query,
    new_kv,
    pool_cache,
    prompt_table,
    prompt_len,
    req_group,
    cont_table,
    cont_len,
    migration,
    diff_lambda,
    out_weight,
    norm_gain,
):
    rows, model = hidden_in.shape
    pages, page_len, width = pool_cache.shape
    span = cont_table.shape[1] * page_len
    slots = MIG_REACH * MIG_CAP
    block = model // n_tp
    smem = pl.BlockSpec(memory_space=pltpu.SMEM)
    vmem = pl.BlockSpec(memory_space=pltpu.VMEM)
    hbm = pl.BlockSpec(memory_space=pl.ANY)
    return pl.pallas_call(
        functools.partial(layer_kernel, n_req, n_tp),
        out_shape=(
            jax.ShapeDtypeStruct((rows, model), BF16),
            jax.ShapeDtypeStruct((rows, model), BF16),
            jax.ShapeDtypeStruct((slots, span, width), BF16),
        ),
        in_specs=[smem] * 7 + [vmem] * 4 + [hbm] * 2,
        out_specs=(vmem, vmem, vmem),
        scratch_shapes=[
            pltpu.VMEM((pages, page_len, width), BF16),
            pltpu.VMEM(out_weight.shape, BF16),
            pltpu.VMEM((rows, width), F32),
            pltpu.VMEM((slots, span, width), BF16),
            pltpu.VMEM((n_tp, rows, block), BF16),
            pltpu.VMEM((n_tp, rows, block), BF16),
            pltpu.VMEM((n_tp, rows, block), BF16),
            pltpu.SemaphoreType.DMA((POOL_CHUNKS,)),
            pltpu.SemaphoreType.DMA,
            pltpu.SemaphoreType.DMA((MIG_REACH,)),
            pltpu.SemaphoreType.DMA((MIG_REACH,)),
            pltpu.SemaphoreType.DMA((n_tp,)),
            pltpu.SemaphoreType.DMA((n_tp,)),
            pltpu.SemaphoreType.DMA((n_tp,)),
            pltpu.SemaphoreType.DMA((n_tp,)),
        ],
        compiler_params=pltpu.CompilerParams(collective_id=0, has_side_effects=True),
        name="decode_layer",
    )(
        prompt_table,
        prompt_len,
        req_group,
        cont_table.T,
        cont_len,
        migration.T,
        diff_lambda,
        hidden_in,
        query,
        new_kv,
        norm_gain.reshape(1, model),
        pool_cache,
        out_weight,
    )


def solution(mesh):
    placed = (
        P("req", None),
        P("req", "tp"),
        P("req", "tp"),
        P("req", None, "tp"),
        P("req", None),
        P("req"),
        P("req"),
        P("req", None),
        P("req"),
        P("req", None),
        P("tp"),
        P("tp", None),
        P(),
    )
    return jax.shard_map(
        functools.partial(shards, mesh.shape["req"], mesh.shape["tp"]),
        mesh=mesh,
        in_specs=placed,
        out_specs=(P("req", None), P("req", None), P("req", None, "tp")),
        check_vma=False,
    )
```

```python
import functools

import jax
import jax.numpy as jnp
from jax import lax
from jax.experimental import pallas as pl
from jax.experimental.pallas import tpu as pltpu
from jax.sharding import PartitionSpec as P

MIG_REACH = 4
MIG_CAP = 2
POOL_CHUNKS = 5
MESH = pl.DeviceIdType.MESH
F32 = jnp.float32
BF16 = jnp.bfloat16
NEG = -1e30


def layer_kernel(
    n_req,
    n_tp,
    prompt_table_hbm,
    prompt_len_hbm,
    req_group_hbm,
    cont_table_hbm,
    cont_len_hbm,
    migration_hbm,
    diff_lambda_hbm,
    hidden_in_hbm,
    query_hbm,
    new_kv_hbm,
    norm_gain_hbm,
    pool_hbm,
    weight_hbm,
    hidden_out,
    normed_out,
    arrived,
    prompt_table,
    prompt_len,
    req_group,
    cont_table,
    cont_len,
    migration,
    diff_lambda,
    hidden_in,
    query,
    new_kv,
    norm_gain,
    pool,
    weight,
    new_rows,
    outgoing,
    part,
    sum_in,
    total,
    small_sem,
    pool_sem,
    weight_sem,
    mig_send,
    mig_recv,
    sum_send,
    sum_recv,
    all_send,
    all_recv,
):
    rows, key_width = query.shape[0], query.shape[1] // 2
    pages, page_len, width = pool.shape
    value_col = 2 * key_width
    groups, group_pages = prompt_table.shape
    cont_pages = cont_table.shape[0]
    moves = migration.shape[1]
    block = total.shape[2]
    my_req = lax.axis_index("req")
    my_tp = lax.axis_index("tp")

    tables = (
        (migration_hbm, migration),
        (cont_table_hbm, cont_table),
        (cont_len_hbm, cont_len),
        (new_kv_hbm, new_kv),
        (prompt_table_hbm, prompt_table),
        (prompt_len_hbm, prompt_len),
        (req_group_hbm, req_group),
        (diff_lambda_hbm, diff_lambda),
        (query_hbm, query),
        (hidden_in_hbm, hidden_in),
        (norm_gain_hbm, norm_gain),
    )
    small_copies = [
        pltpu.make_async_copy(source, target, small_sem.at[index])
        for index, (source, target) in enumerate(tables)
    ]
    for copy in small_copies[:4]:
        copy.start()
    per_chunk = pages // POOL_CHUNKS
    pool_copies = []
    for chunk in range(POOL_CHUNKS):
        piece = pl.ds(chunk * per_chunk, per_chunk)
        pool_copies.append(
            pltpu.make_async_copy(pool_hbm.at[piece], pool.at[piece], pool_sem.at[chunk])
        )
        pool_copies[-1].start()
    weight_copy = pltpu.make_async_copy(weight_hbm, weight, weight_sem)
    for copy in small_copies[4:]:
        copy.start()
    weight_copy.start()

    barrier = pltpu.get_barrier_semaphore()
    for offset in range(1, MIG_REACH + 1):
        for other in (my_req + offset, my_req + n_req - offset):
            pl.semaphore_signal(
                barrier, inc=1, device_id={"req": lax.rem(other, n_req)}, device_id_type=MESH
            )
    for step in range(1, n_tp):
        pl.semaphore_signal(
            barrier, inc=1, device_id={"tp": lax.rem(my_tp + step, n_tp)}, device_id_type=MESH
        )

    for copy in small_copies[:4]:
        copy.wait()
    new_rows[...] = new_kv[...].astype(F32)
    slot_of = []
    for move in range(moves):
        rank = jnp.int32(0)
        for earlier in range(move):
            rank = rank + (migration[1, earlier] == migration[1, move]).astype(jnp.int32)
        slot_of.append((migration[1, move] - 1) * MIG_CAP + rank)
    page_pos = lax.broadcasted_iota(jnp.int32, (page_len, width), 0)

    for copy in pool_copies:
        copy.wait()

    mig_copies = []
    for offset in range(1, MIG_REACH + 1):
        for place in range(MIG_CAP):
            slot = (offset - 1) * MIG_CAP + place
            request, present = jnp.int32(0), jnp.int32(0)
            for move in range(moves):
                here = slot_of[move] == slot
                request = jnp.where(here, migration[0, move], request)
                present = jnp.where(here, 1, present)
            length = jnp.where(present == 1, cont_len[request], -1)
            new_row = new_rows[pl.ds(request, 1), :]
            for page in range(cont_pages):
                held = pool[cont_table[page, request]].astype(F32)
                pos = page_pos + page * page_len
                kept = jnp.where(pos < length, held, 0.0)
                kept = jnp.where(pos == length, new_row, kept)
                outgoing[slot, page * page_len : (page + 1) * page_len, :] = kept.astype(BF16)
        span = pl.ds((offset - 1) * MIG_CAP, MIG_CAP)
        mig_copies.append(
            pltpu.make_async_remote_copy(
                src_ref=outgoing.at[span],
                dst_ref=arrived.at[span],
                send_sem=mig_send.at[offset - 1],
                recv_sem=mig_recv.at[offset - 1],
                device_id={"req": lax.rem(my_req + offset, n_req)},
                device_id_type=MESH,
            )
        )
    pl.semaphore_wait(barrier, 2 * MIG_REACH + n_tp - 1)
    for copy in reversed(mig_copies):
        copy.start()

    for copy in small_copies[4:]:
        copy.wait()
    tile_pages = 8
    tile = tile_pages * page_len
    group_tiles = group_pages // tile_pages
    cont_rows = tile_pages // cont_pages
    row = lax.broadcasted_iota(jnp.int32, (rows, tile), 0)
    lane = lax.broadcasted_iota(jnp.int32, (rows, tile), 1)
    group_row = jnp.zeros((rows, tile), jnp.int32)
    length_row = jnp.zeros((rows, tile), jnp.int32)
    for request in range(rows):
        group_row = jnp.where(row == request, req_group[request], group_row)
        length_row = jnp.where(row == request, cont_len[request], length_row)

    tiles = []
    for group in range(groups):
        limit = jnp.where(group_row == group, prompt_len[group], 0)
        for part_of in range(group_tiles):
            names = [prompt_table[group, part_of * tile_pages + j] for j in range(tile_pages)]
            tiles.append((names, lane + part_of * tile < limit))
    cont_span = cont_pages * page_len
    for first in range(0, rows, cont_rows):
        names = [
            cont_table[j % cont_pages, first + j // cont_pages] for j in range(tile_pages)
        ]
        start = (row - first) * cont_span
        tiles.append((names, (lane >= start) & (lane < start + length_row)))

    scale = key_width ** (-0.5)
    queries = [query[:, twin * key_width : (twin + 1) * key_width] for twin in range(2)]
    contract_last = (((1,), (1,)), ((), ()))

    def scores(keys, mask, twin):
        product = lax.dot_general(
            queries[twin], keys, contract_last, preferred_element_type=F32
        )
        return jnp.where(mask, product * scale, NEG)

    score_tiles = []
    for names, mask in tiles:
        pair = []
        for twin in range(2):
            cols = slice(twin * key_width, (twin + 1) * key_width)
            keys = jnp.concatenate([pool[name, :, cols] for name in names], axis=0)
            pair.append(scores(keys, mask, twin))
        score_tiles.append(jnp.concatenate(pair, axis=0))
    own = lax.broadcasted_iota(jnp.int32, (rows, rows), 0) == lax.broadcasted_iota(
        jnp.int32, (rows, rows), 1
    )
    new_score = jnp.concatenate(
        [
            scores(new_kv[:, twin * key_width : (twin + 1) * key_width], own, twin)
            for twin in range(2)
        ],
        axis=0,
    )
    peak = functools.reduce(jnp.maximum, score_tiles)
    top = jnp.maximum(
        jnp.max(peak, axis=1, keepdims=True), jnp.max(new_score, axis=1, keepdims=True)
    )
    exp_tiles = [jnp.exp(score - top) for score in score_tiles]
    new_exp = jnp.exp(new_score - top)
    denominator = jnp.sum(sum(exp_tiles), axis=1, keepdims=True) + jnp.sum(
        new_exp, axis=1, keepdims=True
    )
    inverse = 1.0 / denominator
    mixture = jnp.dot(
        (new_exp * inverse).astype(BF16), new_kv[:, value_col:], preferred_element_type=F32
    )
    for (names, _), exp_tile in zip(tiles, exp_tiles):
        values = jnp.concatenate([pool[name, :, value_col:] for name in names], axis=0)
        mixture = mixture + jnp.dot(
            (exp_tile * inverse).astype(BF16), values, preferred_element_type=F32
        )
    difference = mixture[:rows] - diff_lambda[0] * mixture[rows:]
    square = jnp.mean(difference * difference, axis=1, keepdims=True)
    attention = (difference * lax.rsqrt(square + 1e-05) * 0.8).astype(BF16)

    weight_copy.wait()

    def columns(index):
        return pl.ds(pl.multiple_of(index * block, block), block)

    sum_copies = []
    for step in (4, 3, 5, 2, 6, 1, 7):
        peer = lax.rem(my_tp + step, n_tp)
        part[step] = jnp.dot(
            attention, weight[:, columns(peer)], preferred_element_type=F32
        ).astype(BF16)
        copy = pltpu.make_async_remote_copy(
            src_ref=part.at[step],
            dst_ref=sum_in.at[step],
            send_sem=sum_send.at[step],
            recv_sem=sum_recv.at[step],
            device_id={"tp": peer},
            device_id_type=MESH,
        )
        copy.start()
        sum_copies.append((step, copy))
    own_part = jnp.dot(
        attention, weight[:, columns(my_tp)], preferred_element_type=F32
    )
    summed = hidden_in[:, columns(my_tp)].astype(F32) + own_part
    for step, copy in reversed(sum_copies):
        copy.wait_recv()
        summed = summed + sum_in[step].astype(F32)
    total[my_tp] = summed.astype(BF16)
    all_copies = []
    for step in (4, 3, 5, 2, 6, 1, 7):
        peer = lax.rem(my_tp + step, n_tp)
        copy = pltpu.make_async_remote_copy(
            src_ref=total.at[my_tp],
            dst_ref=total.at[my_tp],
            send_sem=all_send.at[step],
            recv_sem=all_recv.at[step],
            device_id={"tp": peer},
            device_id_type=MESH,
        )
        copy.start()
        all_copies.append(copy)
    for copy in reversed(all_copies):
        copy.wait_recv()
    blocks = [total[index].astype(F32) for index in range(n_tp)]
    square_sum = functools.reduce(jnp.add, [value * value for value in blocks])
    mean = jnp.sum(square_sum, axis=1, keepdims=True) / (block * n_tp)
    factor = lax.rsqrt(mean + 1e-05)
    for index, value in enumerate(blocks):
        cols = slice(index * block, (index + 1) * block)
        hidden_out[:, cols] = value.astype(BF16)
        normed_out[:, cols] = (value * factor * norm_gain[:, cols]).astype(BF16)
    for _, copy in sum_copies:
        copy.wait_send()
    for copy in all_copies:
        copy.wait_send()
    for copy in mig_copies:
        copy.wait()


def store_kernel(*refs):
    count = len(refs) // 2
    copies = [
        pltpu.make_async_copy(refs[index], refs[count + index], refs[-1].at[index])
        for index in range(count)
    ]
    for copy in copies:
        copy.start()
    for copy in copies:
        copy.wait()


def shards(
    n_req,
    n_tp,
    hidden_in,
    query,
    new_kv,
    pool_cache,
    prompt_table,
    prompt_len,
    req_group,
    cont_table,
    cont_len,
    migration,
    diff_lambda,
    out_weight,
    norm_gain,
):
    rows, model = hidden_in.shape
    pages, page_len, width = pool_cache.shape
    span = cont_table.shape[1] * page_len
    slots = MIG_REACH * MIG_CAP
    block = model // n_tp
    operands = (
        prompt_table,
        prompt_len,
        req_group,
        cont_table.T,
        cont_len,
        migration.T,
        diff_lambda,
        hidden_in,
        query,
        new_kv,
        norm_gain.reshape(1, model),
        pool_cache,
        out_weight,
    )
    anywhere = pl.BlockSpec(memory_space=pl.ANY)
    vmem = pl.BlockSpec(memory_space=pltpu.VMEM)
    shapes = ((rows, model), (rows, model), (slots, span, width))
    results = pl.pallas_call(
        functools.partial(layer_kernel, n_req, n_tp),
        out_shape=tuple(pltpu.VMEM(shape, BF16) for shape in shapes),
        in_specs=[anywhere] * len(operands),
        out_specs=(vmem,) * len(shapes),
        scratch_shapes=[
            *(pltpu.SMEM(value.shape, value.dtype) for value in operands[:7]),
            *(pltpu.VMEM(value.shape, value.dtype) for value in operands[7:]),
            pltpu.VMEM((rows, width), F32),
            pltpu.VMEM((slots, span, width), BF16),
            pltpu.VMEM((n_tp, rows, block), BF16),
            pltpu.VMEM((n_tp, rows, block), BF16),
            pltpu.VMEM((n_tp, rows, block), BF16),
            pltpu.SemaphoreType.DMA((11,)),
            pltpu.SemaphoreType.DMA((POOL_CHUNKS,)),
            pltpu.SemaphoreType.DMA,
            pltpu.SemaphoreType.DMA((MIG_REACH,)),
            pltpu.SemaphoreType.DMA((MIG_REACH,)),
            pltpu.SemaphoreType.DMA((n_tp,)),
            pltpu.SemaphoreType.DMA((n_tp,)),
            pltpu.SemaphoreType.DMA((n_tp,)),
            pltpu.SemaphoreType.DMA((n_tp,)),
        ],
        compiler_params=pltpu.CompilerParams(collective_id=0, has_side_effects=True),
        name="decode_layer",
    )(*operands)
    return pl.pallas_call(
        store_kernel,
        out_shape=tuple(jax.ShapeDtypeStruct(shape, BF16) for shape in shapes),
        in_specs=[vmem] * len(shapes),
        out_specs=(anywhere,) * len(shapes),
        scratch_shapes=[pltpu.SemaphoreType.DMA((len(shapes),))],
        name="store_results",
    )(*(pltpu.with_memory_space_constraint(value, pltpu.VMEM) for value in results))


def solution(mesh):
    placed = (
        P("req", None),
        P("req", "tp"),
        P("req", "tp"),
        P("req", None, "tp"),
        P("req", None),
        P("req"),
        P("req"),
        P("req", None),
        P("req"),
        P("req", None),
        P("tp"),
        P("tp", None),
        P(),
    )
    return jax.shard_map(
        functools.partial(shards, mesh.shape["req"], mesh.shape["tp"]),
        mesh=mesh,
        in_specs=placed,
        out_specs=(P("req", None), P("req", None), P("req", None, "tp")),
        check_vma=False,
    )
```

```python
import functools

import jax
import jax.numpy as jnp
from jax import lax
from jax.experimental import pallas as pl
from jax.experimental.pallas import tpu as pltpu
from jax.sharding import PartitionSpec as P

MIG_REACH = 4
MIG_CAP = 2
SLOTS = MIG_REACH * MIG_CAP
RELAYS = MIG_CAP
ORDER = (0, 1, 2, 4, 5, 3, 6, 7)
ROW = 4
CONT_PAGES = 2
POOL_CHUNKS = 5
MESH = pl.DeviceIdType.MESH
F32 = jnp.float32
BF16 = jnp.bfloat16
NEG = -1e30


def layer_kernel(
    n_req,
    n_tp,
    prompt_table_hbm,
    prompt_len_hbm,
    req_group_hbm,
    cont_table_hbm,
    cont_len_hbm,
    migration_hbm,
    diff_lambda_hbm,
    hidden_in_hbm,
    query_hbm,
    new_kv_hbm,
    norm_gain_hbm,
    pool_hbm,
    weight_hbm,
    hidden_out,
    normed_out,
    arrived,
    prompt_table,
    prompt_len,
    req_group,
    cont_table,
    cont_len,
    migration,
    diff_lambda,
    hidden_in,
    query,
    new_kv,
    norm_gain,
    pool,
    weight,
    new_rows,
    mixed,
    outgoing,
    part,
    sum_in,
    total,
    small_sem,
    pool_sem,
    weight_sem,
    mig_send,
    mig_recv,
    sum_send,
    sum_recv,
    all_send,
    all_recv,
):
    rows, key_width = query.shape[0], query.shape[1] // 2
    pages, page_len, width = pool.shape
    value_col = 2 * key_width
    groups, group_pages = prompt_table.shape
    cont_pages = cont_table.shape[0]
    moves = migration.shape[1]
    block = total.shape[2]
    my_req = lax.axis_index("req")
    my_tp = lax.axis_index("tp")

    tables = (
        (migration_hbm, migration),
        (cont_table_hbm, cont_table),
        (cont_len_hbm, cont_len),
        (new_kv_hbm, new_kv),
        (prompt_table_hbm, prompt_table),
        (prompt_len_hbm, prompt_len),
        (req_group_hbm, req_group),
        (diff_lambda_hbm, diff_lambda),
        (query_hbm, query),
        (hidden_in_hbm, hidden_in),
        (norm_gain_hbm, norm_gain),
    )
    small_copies = [
        pltpu.make_async_copy(source, target, small_sem.at[index])
        for index, (source, target) in enumerate(tables)
    ]
    for copy in small_copies[:4]:
        copy.start()
    per_chunk = pages // POOL_CHUNKS
    pool_copies = []
    for chunk in range(POOL_CHUNKS):
        piece = pl.ds(chunk * per_chunk, per_chunk)
        pool_copies.append(
            pltpu.make_async_copy(pool_hbm.at[piece], pool.at[piece], pool_sem.at[chunk])
        )
        pool_copies[-1].start()
    weight_copy = pltpu.make_async_copy(weight_hbm, weight, weight_sem)
    for copy in small_copies[4:]:
        copy.start()
    weight_copy.start()

    barrier = pltpu.get_barrier_semaphore()
    for offset in range(1, MIG_REACH + 1):
        for other in (my_req + offset, my_req + n_req - offset):
            pl.semaphore_signal(
                barrier, inc=1, device_id={"req": lax.rem(other, n_req)}, device_id_type=MESH
            )
    for step in range(1, n_tp):
        pl.semaphore_signal(
            barrier, inc=1, device_id={"tp": lax.rem(my_tp + step, n_tp)}, device_id_type=MESH
        )

    for copy in small_copies[:4]:
        copy.wait()
    new_rows[...] = new_kv[...].astype(F32)
    slot_of = []
    for move in range(moves):
        rank = jnp.int32(0)
        for earlier in range(move):
            rank = rank + (migration[1, earlier] == migration[1, move]).astype(jnp.int32)
        slot_of.append((migration[1, move] - 1) * MIG_CAP + rank)
    page_pos = lax.broadcasted_iota(jnp.int32, (page_len, width), 0)

    for copy in pool_copies:
        copy.wait()

    my_y = lax.rem(my_req, ROW)
    far = (my_y == ROW - 1).astype(jnp.int32)

    def send_pages():
        pl.semaphore_wait(barrier, 2 * MIG_REACH + n_tp - 1)
        for slot in ORDER:
            offset = slot // MIG_CAP + 1
            request, present = jnp.int32(0), jnp.int32(0)
            for move in range(moves):
                here = slot_of[move] == slot
                request = jnp.where(here, migration[0, move], request)
                present = jnp.where(here, 1, present)
            length = jnp.where(present == 1, cont_len[request], -1)
            new_row = new_rows[pl.ds(request, 1), :]
            relayed = far if offset == 1 else 0
            target = lax.rem(my_req + n_req + offset - ROW * relayed, n_req)
            place = slot + SLOTS * relayed
            for page in range(cont_pages):
                held = pool[cont_table[page, request]].astype(F32)
                pos = page_pos + page * page_len
                kept = jnp.where(pos < length, held, 0.0)
                kept = jnp.where(pos == length, new_row, kept)
                span = pl.ds(page * page_len, page_len)
                outgoing[slot, span, :] = kept.astype(BF16)
                pltpu.make_async_remote_copy(
                    src_ref=outgoing.at[slot, span],
                    dst_ref=arrived.at[place, span],
                    send_sem=mig_send.at[slot],
                    recv_sem=mig_recv.at[slot + relayed * (SLOTS + slot + page)],
                    device_id={"req": target},
                    device_id_type=MESH,
                ).start()

    def attend():
        for copy in small_copies[4:]:
            copy.wait()
        tile_pages = 8
        tile = tile_pages * page_len
        group_tiles = group_pages // tile_pages
        cont_rows = tile_pages // cont_pages
        row = lax.broadcasted_iota(jnp.int32, (rows, tile), 0)
        lane = lax.broadcasted_iota(jnp.int32, (rows, tile), 1)
        group_row = jnp.zeros((rows, tile), jnp.int32)
        length_row = jnp.zeros((rows, tile), jnp.int32)
        for request in range(rows):
            group_row = jnp.where(row == request, req_group[request], group_row)
            length_row = jnp.where(row == request, cont_len[request], length_row)

        tiles = []
        for group in range(groups):
            limit = jnp.where(group_row == group, prompt_len[group], 0)
            for part_of in range(group_tiles):
                names = [prompt_table[group, part_of * tile_pages + j] for j in range(tile_pages)]
                tiles.append((names, lane + part_of * tile < limit))
        cont_span = cont_pages * page_len
        for first in range(0, rows, cont_rows):
            names = [
                cont_table[j % cont_pages, first + j // cont_pages] for j in range(tile_pages)
            ]
            start = (row - first) * cont_span
            tiles.append((names, (lane >= start) & (lane < start + length_row)))

        scale = key_width ** (-0.5)
        queries = [query[:, twin * key_width : (twin + 1) * key_width] for twin in range(2)]
        contract_last = (((1,), (1,)), ((), ()))

        def scores(keys, mask, twin):
            product = lax.dot_general(
                queries[twin], keys, contract_last, preferred_element_type=F32
            )
            return jnp.where(mask, product * scale, NEG)

        score_tiles = []
        for names, mask in tiles:
            pair = []
            for twin in range(2):
                cols = slice(twin * key_width, (twin + 1) * key_width)
                keys = jnp.concatenate([pool[name, :, cols] for name in names], axis=0)
                pair.append(scores(keys, mask, twin))
            score_tiles.append(jnp.concatenate(pair, axis=0))
        own = lax.broadcasted_iota(jnp.int32, (rows, rows), 0) == lax.broadcasted_iota(
            jnp.int32, (rows, rows), 1
        )
        new_score = jnp.concatenate(
            [
                scores(new_kv[:, twin * key_width : (twin + 1) * key_width], own, twin)
                for twin in range(2)
            ],
            axis=0,
        )
        peak = functools.reduce(jnp.maximum, score_tiles)
        top = jnp.maximum(
            jnp.max(peak, axis=1, keepdims=True), jnp.max(new_score, axis=1, keepdims=True)
        )
        exp_tiles = [jnp.exp(score - top) for score in score_tiles]
        new_exp = jnp.exp(new_score - top)
        denominator = jnp.sum(sum(exp_tiles), axis=1, keepdims=True) + jnp.sum(
            new_exp, axis=1, keepdims=True
        )
        inverse = 1.0 / denominator
        mixture = jnp.dot(
            (new_exp * inverse).astype(BF16), new_kv[:, value_col:], preferred_element_type=F32
        )
        for (names, _), exp_tile in zip(tiles, exp_tiles):
            values = jnp.concatenate([pool[name, :, value_col:] for name in names], axis=0)
            mixture = mixture + jnp.dot(
                (exp_tile * inverse).astype(BF16), values, preferred_element_type=F32
            )
        difference = mixture[:rows] - diff_lambda[0] * mixture[rows:]
        square = jnp.mean(difference * difference, axis=1, keepdims=True)
        mixed[...] = (difference * lax.rsqrt(square + 1e-05) * 0.8).astype(BF16)


    early = my_req < ROW

    @pl.loop(0, 2)
    def _(phase):
        pl.when((phase == 0) == early)(attend)
        pl.when((phase == 0) != early)(send_pages)

    def relay(slot, page):
        span = pl.ds(page * page_len, page_len)
        return pltpu.make_async_remote_copy(
            src_ref=arrived.at[SLOTS + slot, span],
            dst_ref=arrived.at[slot, span],
            send_sem=mig_send.at[SLOTS + slot],
            recv_sem=mig_recv.at[slot],
            device_id={"req": lax.rem(my_req + ROW, n_req)},
            device_id_type=MESH,
        )

    def wait_bytes(ref, sem):
        pltpu.make_async_copy(ref, ref, sem).wait()

    def pass_on():
        for slot in range(MIG_CAP):
            for page in range(cont_pages):
                span = pl.ds(page * page_len, page_len)
                wait_bytes(
                    arrived.at[SLOTS + slot, span], mig_recv.at[SLOTS + 2 * slot + page]
                )
                relay(slot, page).start()

    attention = mixed[...]
    weight_copy.wait()

    def columns(index):
        return pl.ds(pl.multiple_of(index * block, block), block)

    sum_copies = []
    for step in (4, 3, 5, 2, 6, 1, 7):
        peer = lax.rem(my_tp + step, n_tp)
        part[step] = jnp.dot(
            attention, weight[:, columns(peer)], preferred_element_type=F32
        ).astype(BF16)
        copy = pltpu.make_async_remote_copy(
            src_ref=part.at[step],
            dst_ref=sum_in.at[step],
            send_sem=sum_send.at[step],
            recv_sem=sum_recv.at[step],
            device_id={"tp": peer},
            device_id_type=MESH,
        )
        copy.start()
        sum_copies.append((step, copy))
    pl.when(my_y == 0)(pass_on)
    own_part = jnp.dot(
        attention, weight[:, columns(my_tp)], preferred_element_type=F32
    )
    summed = hidden_in[:, columns(my_tp)].astype(F32) + own_part
    for step, copy in reversed(sum_copies):
        copy.wait_recv()
        summed = summed + sum_in[step].astype(F32)
    total[my_tp] = summed.astype(BF16)
    all_copies = []
    for step in (4, 3, 5, 2, 6, 1, 7):
        peer = lax.rem(my_tp + step, n_tp)
        copy = pltpu.make_async_remote_copy(
            src_ref=total.at[my_tp],
            dst_ref=total.at[my_tp],
            send_sem=all_send.at[step],
            recv_sem=all_recv.at[step],
            device_id={"tp": peer},
            device_id_type=MESH,
        )
        copy.start()
        all_copies.append(copy)
    for copy in reversed(all_copies):
        copy.wait_recv()
    blocks = [total[index].astype(F32) for index in range(n_tp)]
    square_sum = functools.reduce(jnp.add, [value * value for value in blocks])
    mean = jnp.sum(square_sum, axis=1, keepdims=True) / (block * n_tp)
    factor = lax.rsqrt(mean + 1e-05)
    for index, value in enumerate(blocks):
        cols = slice(index * block, (index + 1) * block)
        hidden_out[:, cols] = value.astype(BF16)
        normed_out[:, cols] = (value * factor * norm_gain[:, cols]).astype(BF16)
    for _, copy in sum_copies:
        copy.wait_send()
    for copy in all_copies:
        copy.wait_send()
    for slot in range(SLOTS):
        wait_bytes(outgoing.at[slot], mig_send.at[slot])
        wait_bytes(arrived.at[slot], mig_recv.at[slot])

    @pl.when(my_y == 0)
    def _():
        for slot in range(MIG_CAP):
            wait_bytes(arrived.at[SLOTS + slot], mig_send.at[SLOTS + slot])


def store_kernel(*refs):
    count = len(refs) // 2
    copies = [
        pltpu.make_async_copy(
            refs[index].at[pl.ds(0, refs[count + index].shape[0])],
            refs[count + index],
            refs[-1].at[index],
        )
        for index in range(count)
    ]
    for copy in copies:
        copy.start()
    for copy in copies:
        copy.wait()


def shards(
    n_req,
    n_tp,
    hidden_in,
    query,
    new_kv,
    pool_cache,
    prompt_table,
    prompt_len,
    req_group,
    cont_table,
    cont_len,
    migration,
    diff_lambda,
    out_weight,
    norm_gain,
):
    rows, model = hidden_in.shape
    pages, page_len, width = pool_cache.shape
    span = cont_table.shape[1] * page_len
    block = model // n_tp
    operands = (
        prompt_table,
        prompt_len,
        req_group,
        cont_table.T,
        cont_len,
        migration.T,
        diff_lambda,
        hidden_in,
        query,
        new_kv,
        norm_gain.reshape(1, model),
        pool_cache,
        out_weight,
    )
    anywhere = pl.BlockSpec(memory_space=pl.ANY)
    vmem = pl.BlockSpec(memory_space=pltpu.VMEM)
    shapes = ((rows, model), (rows, model), (SLOTS, span, width))
    landing = ((rows, model), (rows, model), (SLOTS + RELAYS, span, width))
    results = pl.pallas_call(
        functools.partial(layer_kernel, n_req, n_tp),
        out_shape=tuple(pltpu.VMEM(shape, BF16) for shape in landing),
        in_specs=[anywhere] * len(operands),
        out_specs=(vmem,) * len(shapes),
        scratch_shapes=[
            *(pltpu.SMEM(value.shape, value.dtype) for value in operands[:7]),
            *(pltpu.VMEM(value.shape, value.dtype) for value in operands[7:]),
            pltpu.VMEM((rows, width), F32),
            pltpu.VMEM((rows, out_weight.shape[0]), BF16),
            pltpu.VMEM((SLOTS, span, width), BF16),
            pltpu.VMEM((n_tp, rows, block), BF16),
            pltpu.VMEM((n_tp, rows, block), BF16),
            pltpu.VMEM((n_tp, rows, block), BF16),
            pltpu.SemaphoreType.DMA((11,)),
            pltpu.SemaphoreType.DMA((POOL_CHUNKS,)),
            pltpu.SemaphoreType.DMA,
            pltpu.SemaphoreType.DMA((SLOTS + RELAYS,)),
            pltpu.SemaphoreType.DMA((SLOTS + RELAYS * CONT_PAGES,)),
            pltpu.SemaphoreType.DMA((n_tp,)),
            pltpu.SemaphoreType.DMA((n_tp,)),
            pltpu.SemaphoreType.DMA((n_tp,)),
            pltpu.SemaphoreType.DMA((n_tp,)),
        ],
        compiler_params=pltpu.CompilerParams(collective_id=0, has_side_effects=True),
        name="decode_layer",
    )(*operands)
    return pl.pallas_call(
        store_kernel,
        out_shape=tuple(jax.ShapeDtypeStruct(shape, BF16) for shape in shapes),
        in_specs=[vmem] * len(shapes),
        out_specs=(anywhere,) * len(shapes),
        scratch_shapes=[pltpu.SemaphoreType.DMA((len(shapes),))],
        name="store_results",
    )(*(pltpu.with_memory_space_constraint(value, pltpu.VMEM) for value in results))


def solution(mesh):
    placed = (
        P("req", None),
        P("req", "tp"),
        P("req", "tp"),
        P("req", None, "tp"),
        P("req", None),
        P("req"),
        P("req"),
        P("req", None),
        P("req"),
        P("req", None),
        P("tp"),
        P("tp", None),
        P(),
    )
    return jax.shard_map(
        functools.partial(shards, mesh.shape["req"], mesh.shape["tp"]),
        mesh=mesh,
        in_specs=placed,
        out_specs=(P("req", None), P("req", None), P("req", None, "tp")),
        check_vma=False,
    )
```

```python
import functools

import jax
import jax.numpy as jnp
from jax import lax
from jax.experimental import pallas as pl
from jax.experimental.pallas import tpu as pltpu
from jax.sharding import PartitionSpec as P

MIG_REACH = 4
MIG_CAP = 2
SLOTS = MIG_REACH * MIG_CAP
RELAYS = MIG_CAP
ROW = 4
CONT_PAGES = 2
POOL_CHUNKS = 5
MESH = pl.DeviceIdType.MESH
F32 = jnp.float32
BF16 = jnp.bfloat16
NEG = -1e30


def layer_kernel(
    n_req,
    n_tp,
    prompt_table_hbm,
    prompt_len_hbm,
    req_group_hbm,
    cont_table_hbm,
    cont_len_hbm,
    migration_hbm,
    diff_lambda_hbm,
    hidden_in_hbm,
    query_hbm,
    new_kv_hbm,
    norm_gain_hbm,
    pool_hbm,
    weight_hbm,
    hidden_out,
    normed_out,
    arrived,
    prompt_table,
    prompt_len,
    req_group,
    cont_table,
    cont_len,
    migration,
    diff_lambda,
    hidden_in,
    query,
    new_kv,
    norm_gain,
    pool,
    weight,
    new_rows,
    mixed,
    outgoing,
    part,
    sum_in,
    total,
    small_sem,
    pool_sem,
    weight_sem,
    mig_send,
    mig_recv,
    sum_send,
    sum_recv,
    all_send,
    all_recv,
):
    rows, key_width = query.shape[0], query.shape[1] // 2
    pages, page_len, width = pool.shape
    value_col = 2 * key_width
    groups, group_pages = prompt_table.shape
    cont_pages = cont_table.shape[0]
    moves = migration.shape[1]
    block = total.shape[2]
    my_req = lax.axis_index("req")
    my_tp = lax.axis_index("tp")

    tables = (
        (migration_hbm, migration),
        (cont_table_hbm, cont_table),
        (cont_len_hbm, cont_len),
        (new_kv_hbm, new_kv),
        (prompt_table_hbm, prompt_table),
        (prompt_len_hbm, prompt_len),
        (req_group_hbm, req_group),
        (diff_lambda_hbm, diff_lambda),
        (query_hbm, query),
        (hidden_in_hbm, hidden_in),
        (norm_gain_hbm, norm_gain),
    )
    small_copies = [
        pltpu.make_async_copy(source, target, small_sem.at[index])
        for index, (source, target) in enumerate(tables)
    ]
    for copy in small_copies[:4]:
        copy.start()
    per_chunk = pages // POOL_CHUNKS
    pool_copies = []
    for chunk in range(POOL_CHUNKS):
        piece = pl.ds(chunk * per_chunk, per_chunk)
        pool_copies.append(
            pltpu.make_async_copy(pool_hbm.at[piece], pool.at[piece], pool_sem.at[chunk])
        )
        pool_copies[-1].start()
    weight_copy = pltpu.make_async_copy(weight_hbm, weight, weight_sem)
    for copy in small_copies[4:]:
        copy.start()

    barrier = pltpu.get_barrier_semaphore()
    my_y = lax.rem(my_req, ROW)
    far = (my_y == ROW - 1).astype(jnp.int32)
    near = (my_y == 1).astype(jnp.int32)
    for offset in range(1, MIG_REACH + 1):
        source = my_req + n_req - offset
        if offset == 2:
            source = source + ROW * near
        pl.semaphore_signal(
            barrier, inc=1, device_id={"req": lax.rem(source, n_req)}, device_id_type=MESH
        )
    for step in range(1, n_tp):
        pl.semaphore_signal(
            barrier, inc=1, device_id={"tp": lax.rem(my_tp + step, n_tp)}, device_id_type=MESH
        )

    for copy in small_copies[:4]:
        copy.wait()
    new_rows[...] = new_kv[...].astype(F32)
    slot_of = []
    for move in range(moves):
        rank = jnp.int32(0)
        for earlier in range(move):
            rank = rank + (migration[1, earlier] == migration[1, move]).astype(jnp.int32)
        slot_of.append((migration[1, move] - 1) * MIG_CAP + rank)
    page_pos = lax.broadcasted_iota(jnp.int32, (page_len, width), 0)

    for copy in pool_copies:
        copy.wait()
    weight_copy.start()

    def send_pages():
        pl.semaphore_wait(barrier, MIG_REACH + n_tp - 1)
        first = MIG_CAP * (ROW - 1 - my_y)
        for turn in range(SLOTS):
            slot = lax.rem(first + turn, SLOTS)
            offset = lax.div(slot, MIG_CAP) + 1
            request, present = jnp.int32(0), jnp.int32(0)
            for move in range(moves):
                here = slot_of[move] == slot
                request = jnp.where(here, migration[0, move], request)
                present = jnp.where(here, 1, present)
            length = jnp.where(present == 1, cont_len[request], -1)
            new_row = new_rows[pl.ds(request, 1), :]
            relayed = far if turn // MIG_CAP == 1 else 0
            target = lax.rem(my_req + n_req + offset - ROW * relayed, n_req)
            place = slot + (SLOTS - MIG_CAP) * relayed
            for page in range(cont_pages):
                held = pool[cont_table[page, request]].astype(F32)
                pos = page_pos + page * page_len
                kept = jnp.where(pos < length, held, 0.0)
                kept = jnp.where(pos == length, new_row, kept)
                span = pl.ds(page * page_len, page_len)
                outgoing[slot, span, :] = kept.astype(BF16)
                pltpu.make_async_remote_copy(
                    src_ref=outgoing.at[slot, span],
                    dst_ref=arrived.at[place, span],
                    send_sem=mig_send.at[slot],
                    recv_sem=mig_recv.at[slot + relayed * (SLOTS - 2 * MIG_CAP + slot + page)],
                    device_id={"req": target},
                    device_id_type=MESH,
                ).start()

    def attend():
        for copy in small_copies[4:]:
            copy.wait()
        tile_pages = 8
        tile = tile_pages * page_len
        group_tiles = group_pages // tile_pages
        cont_rows = tile_pages // cont_pages
        row = lax.broadcasted_iota(jnp.int32, (rows, tile), 0)
        lane = lax.broadcasted_iota(jnp.int32, (rows, tile), 1)
        group_row = jnp.zeros((rows, tile), jnp.int32)
        length_row = jnp.zeros((rows, tile), jnp.int32)
        for request in range(rows):
            group_row = jnp.where(row == request, req_group[request], group_row)
            length_row = jnp.where(row == request, cont_len[request], length_row)

        tiles = []
        for group in range(groups):
            limit = jnp.where(group_row == group, prompt_len[group], 0)
            for part_of in range(group_tiles):
                names = [prompt_table[group, part_of * tile_pages + j] for j in range(tile_pages)]
                tiles.append((names, lane + part_of * tile < limit))
        cont_span = cont_pages * page_len
        for first in range(0, rows, cont_rows):
            names = [
                cont_table[j % cont_pages, first + j // cont_pages] for j in range(tile_pages)
            ]
            start = (row - first) * cont_span
            tiles.append((names, (lane >= start) & (lane < start + length_row)))

        scale = key_width ** (-0.5)
        queries = [query[:, twin * key_width : (twin + 1) * key_width] for twin in range(2)]
        contract_last = (((1,), (1,)), ((), ()))

        def scores(keys, mask, twin):
            product = lax.dot_general(
                queries[twin], keys, contract_last, preferred_element_type=F32
            )
            return jnp.where(mask, product * scale, NEG)

        score_tiles = []
        for names, mask in tiles:
            pair = []
            for twin in range(2):
                cols = slice(twin * key_width, (twin + 1) * key_width)
                keys = jnp.concatenate([pool[name, :, cols] for name in names], axis=0)
                pair.append(scores(keys, mask, twin))
            score_tiles.append(jnp.concatenate(pair, axis=0))
        own = lax.broadcasted_iota(jnp.int32, (rows, rows), 0) == lax.broadcasted_iota(
            jnp.int32, (rows, rows), 1
        )
        new_score = jnp.concatenate(
            [
                scores(new_kv[:, twin * key_width : (twin + 1) * key_width], own, twin)
                for twin in range(2)
            ],
            axis=0,
        )
        peak = functools.reduce(jnp.maximum, score_tiles)
        top = jnp.maximum(
            jnp.max(peak, axis=1, keepdims=True), jnp.max(new_score, axis=1, keepdims=True)
        )
        exp_tiles = [jnp.exp(score - top) for score in score_tiles]
        new_exp = jnp.exp(new_score - top)
        denominator = jnp.sum(sum(exp_tiles), axis=1, keepdims=True) + jnp.sum(
            new_exp, axis=1, keepdims=True
        )
        inverse = 1.0 / denominator
        mixture = jnp.dot(
            (new_exp * inverse).astype(BF16), new_kv[:, value_col:], preferred_element_type=F32
        )
        for (names, _), exp_tile in zip(tiles, exp_tiles):
            values = jnp.concatenate([pool[name, :, value_col:] for name in names], axis=0)
            mixture = mixture + jnp.dot(
                (exp_tile * inverse).astype(BF16), values, preferred_element_type=F32
            )
        difference = mixture[:rows] - diff_lambda[0] * mixture[rows:]
        square = jnp.mean(difference * difference, axis=1, keepdims=True)
        mixed[...] = (difference * lax.rsqrt(square + 1e-05) * 0.8).astype(BF16)


    send_pages()
    attend()

    def relay(slot, page):
        span = pl.ds(page * page_len, page_len)
        return pltpu.make_async_remote_copy(
            src_ref=arrived.at[SLOTS + slot, span],
            dst_ref=arrived.at[MIG_CAP + slot, span],
            send_sem=mig_send.at[SLOTS + slot],
            recv_sem=mig_recv.at[MIG_CAP + slot],
            device_id={"req": lax.rem(my_req + ROW, n_req)},
            device_id_type=MESH,
        )

    def wait_bytes(ref, sem):
        pltpu.make_async_copy(ref, ref, sem).wait()

    def pass_on():
        for slot in range(MIG_CAP):
            for page in range(cont_pages):
                span = pl.ds(page * page_len, page_len)
                wait_bytes(
                    arrived.at[SLOTS + slot, span], mig_recv.at[SLOTS + 2 * slot + page]
                )
                relay(slot, page).start()

    attention = mixed[...]
    weight_copy.wait()

    def columns(index):
        return pl.ds(pl.multiple_of(index * block, block), block)

    sum_copies = []
    for step in (4, 3, 5, 2, 6, 1, 7):
        peer = lax.rem(my_tp + step, n_tp)
        part[step] = jnp.dot(
            attention, weight[:, columns(peer)], preferred_element_type=F32
        ).astype(BF16)
        copy = pltpu.make_async_remote_copy(
            src_ref=part.at[step],
            dst_ref=sum_in.at[step],
            send_sem=sum_send.at[step],
            recv_sem=sum_recv.at[step],
            device_id={"tp": peer},
            device_id_type=MESH,
        )
        copy.start()
        sum_copies.append((step, copy))
    pl.when(my_y == 1)(pass_on)
    own_part = jnp.dot(
        attention, weight[:, columns(my_tp)], preferred_element_type=F32
    )
    summed = hidden_in[:, columns(my_tp)].astype(F32) + own_part
    for step, copy in reversed(sum_copies):
        copy.wait_recv()
        summed = summed + sum_in[step].astype(F32)
    total[my_tp] = summed.astype(BF16)
    all_copies = []
    for step in (4, 3, 5, 2, 6, 1, 7):
        peer = lax.rem(my_tp + step, n_tp)
        copy = pltpu.make_async_remote_copy(
            src_ref=total.at[my_tp],
            dst_ref=total.at[my_tp],
            send_sem=all_send.at[step],
            recv_sem=all_recv.at[step],
            device_id={"tp": peer},
            device_id_type=MESH,
        )
        copy.start()
        all_copies.append(copy)
    for copy in reversed(all_copies):
        copy.wait_recv()
    blocks = [total[index].astype(F32) for index in range(n_tp)]
    square_sum = functools.reduce(jnp.add, [value * value for value in blocks])
    mean = jnp.sum(square_sum, axis=1, keepdims=True) / (block * n_tp)
    factor = lax.rsqrt(mean + 1e-05)
    for index, value in enumerate(blocks):
        cols = slice(index * block, (index + 1) * block)
        hidden_out[:, cols] = value.astype(BF16)
        normed_out[:, cols] = (value * factor * norm_gain[:, cols]).astype(BF16)
    for _, copy in sum_copies:
        copy.wait_send()
    for copy in all_copies:
        copy.wait_send()
    for slot in range(SLOTS):
        wait_bytes(outgoing.at[slot], mig_send.at[slot])
        wait_bytes(arrived.at[slot], mig_recv.at[slot])

    @pl.when(my_y == 1)
    def _():
        for slot in range(MIG_CAP):
            wait_bytes(arrived.at[SLOTS + slot], mig_send.at[SLOTS + slot])


def store_kernel(*refs):
    count = len(refs) // 2
    copies = [
        pltpu.make_async_copy(
            refs[index].at[pl.ds(0, refs[count + index].shape[0])],
            refs[count + index],
            refs[-1].at[index],
        )
        for index in range(count)
    ]
    for copy in copies:
        copy.start()
    for copy in copies:
        copy.wait()


def shards(
    n_req,
    n_tp,
    hidden_in,
    query,
    new_kv,
    pool_cache,
    prompt_table,
    prompt_len,
    req_group,
    cont_table,
    cont_len,
    migration,
    diff_lambda,
    out_weight,
    norm_gain,
):
    rows, model = hidden_in.shape
    pages, page_len, width = pool_cache.shape
    span = cont_table.shape[1] * page_len
    block = model // n_tp
    operands = (
        prompt_table,
        prompt_len,
        req_group,
        cont_table.T,
        cont_len,
        migration.T,
        diff_lambda,
        hidden_in,
        query,
        new_kv,
        norm_gain.reshape(1, model),
        pool_cache,
        out_weight,
    )
    anywhere = pl.BlockSpec(memory_space=pl.ANY)
    vmem = pl.BlockSpec(memory_space=pltpu.VMEM)
    shapes = ((rows, model), (rows, model), (SLOTS, span, width))
    landing = ((rows, model), (rows, model), (SLOTS + RELAYS, span, width))
    results = pl.pallas_call(
        functools.partial(layer_kernel, n_req, n_tp),
        out_shape=tuple(pltpu.VMEM(shape, BF16) for shape in landing),
        in_specs=[anywhere] * len(operands),
        out_specs=(vmem,) * len(shapes),
        scratch_shapes=[
            *(pltpu.SMEM(value.shape, value.dtype) for value in operands[:7]),
            *(pltpu.VMEM(value.shape, value.dtype) for value in operands[7:]),
            pltpu.VMEM((rows, width), F32),
            pltpu.VMEM((rows, out_weight.shape[0]), BF16),
            pltpu.VMEM((SLOTS, span, width), BF16),
            pltpu.VMEM((n_tp, rows, block), BF16),
            pltpu.VMEM((n_tp, rows, block), BF16),
            pltpu.VMEM((n_tp, rows, block), BF16),
            pltpu.SemaphoreType.DMA((11,)),
            pltpu.SemaphoreType.DMA((POOL_CHUNKS,)),
            pltpu.SemaphoreType.DMA,
            pltpu.SemaphoreType.DMA((SLOTS + RELAYS,)),
            pltpu.SemaphoreType.DMA((SLOTS + RELAYS * CONT_PAGES,)),
            pltpu.SemaphoreType.DMA((n_tp,)),
            pltpu.SemaphoreType.DMA((n_tp,)),
            pltpu.SemaphoreType.DMA((n_tp,)),
            pltpu.SemaphoreType.DMA((n_tp,)),
        ],
        compiler_params=pltpu.CompilerParams(collective_id=0, has_side_effects=True),
        name="decode_layer",
    )(*operands)
    return pl.pallas_call(
        store_kernel,
        out_shape=tuple(jax.ShapeDtypeStruct(shape, BF16) for shape in shapes),
        in_specs=[vmem] * len(shapes),
        out_specs=(anywhere,) * len(shapes),
        scratch_shapes=[pltpu.SemaphoreType.DMA((len(shapes),))],
        name="store_results",
    )(*(pltpu.with_memory_space_constraint(value, pltpu.VMEM) for value in results))


def solution(mesh):
    placed = (
        P("req", None),
        P("req", "tp"),
        P("req", "tp"),
        P("req", None, "tp"),
        P("req", None),
        P("req"),
        P("req"),
        P("req", None),
        P("req"),
        P("req", None),
        P("tp"),
        P("tp", None),
        P(),
    )
    return jax.shard_map(
        functools.partial(shards, mesh.shape["req"], mesh.shape["tp"]),
        mesh=mesh,
        in_specs=placed,
        out_specs=(P("req", None), P("req", None), P("req", None, "tp")),
        check_vma=False,
    )
```

```python
import functools

import jax
import jax.numpy as jnp
from jax import lax
from jax.experimental import pallas as pl
from jax.experimental.pallas import tpu as pltpu
from jax.sharding import PartitionSpec as P

MIG_REACH = 4
MIG_CAP = 2
SLOTS = MIG_REACH * MIG_CAP
RELAYS = MIG_CAP
ROW = 4
CONT_PAGES = 2
POOL_CHUNKS = 5
MESH = pl.DeviceIdType.MESH
F32 = jnp.float32
BF16 = jnp.bfloat16
NEG = -1e30


def layer_kernel(
    n_req,
    n_tp,
    prompt_table_hbm,
    prompt_len_hbm,
    req_group_hbm,
    cont_table_hbm,
    cont_len_hbm,
    migration_hbm,
    diff_lambda_hbm,
    hidden_in_hbm,
    query_hbm,
    new_kv_hbm,
    norm_gain_hbm,
    pool_hbm,
    weight_hbm,
    hidden_out,
    normed_out,
    arrived,
    prompt_table,
    prompt_len,
    req_group,
    cont_table,
    cont_len,
    migration,
    diff_lambda,
    hidden_in,
    query,
    new_kv,
    norm_gain,
    pool,
    weight,
    new_rows,
    mixed,
    outgoing,
    part,
    sum_in,
    total,
    ready,
    small_sem,
    pool_sem,
    weight_sem,
    mig_send,
    mig_recv,
    sum_send,
    sum_recv,
    all_send,
    all_recv,
):
    rows, key_width = query.shape[0], query.shape[1] // 2
    pages, page_len, width = pool.shape
    value_col = 2 * key_width
    groups, group_pages = prompt_table.shape
    cont_pages = cont_table.shape[0]
    moves = migration.shape[1]
    block = total.shape[2]
    my_req = lax.axis_index("req")
    my_tp = lax.axis_index("tp")

    tables = (
        (migration_hbm, migration),
        (cont_table_hbm, cont_table),
        (cont_len_hbm, cont_len),
        (new_kv_hbm, new_kv),
        (prompt_table_hbm, prompt_table),
        (prompt_len_hbm, prompt_len),
        (req_group_hbm, req_group),
        (diff_lambda_hbm, diff_lambda),
        (query_hbm, query),
        (hidden_in_hbm, hidden_in),
        (norm_gain_hbm, norm_gain),
    )
    small_copies = [
        pltpu.make_async_copy(source, target, small_sem.at[index])
        for index, (source, target) in enumerate(tables)
    ]
    for copy in small_copies[:4]:
        copy.start()
    per_chunk = pages // POOL_CHUNKS
    pool_copies = []
    for chunk in range(POOL_CHUNKS):
        piece = pl.ds(chunk * per_chunk, per_chunk)
        pool_copies.append(
            pltpu.make_async_copy(pool_hbm.at[piece], pool.at[piece], pool_sem.at[chunk])
        )
        pool_copies[-1].start()
    weight_copy = pltpu.make_async_copy(weight_hbm, weight, weight_sem)
    for copy in small_copies[4:]:
        copy.start()

    barrier = pltpu.get_barrier_semaphore()
    my_y = lax.rem(my_req, ROW)
    far = (my_y == ROW - 1).astype(jnp.int32)

    def tell(semaphore, axis, index):
        pl.semaphore_signal(
            semaphore, inc=1, device_id={axis: index}, device_id_type=MESH
        )

    def req_at(step):
        return lax.rem(my_req + n_req + step, n_req)

    def tp_at(step):
        return lax.rem(my_tp + n_tp + step, n_tp)

    for offset in range(1, MIG_REACH + 1):
        crosses = my_y < offset
        if offset == 2:
            crosses = crosses & (my_y != 1)
        pl.when(crosses)(functools.partial(tell, barrier, "req", req_at(-offset)))
    for step in range(1, ROW):
        pl.when(my_y + step < ROW)(functools.partial(tell, barrier, "req", req_at(step)))
    for step in range(1, n_tp):
        pl.when(my_tp + step < n_tp)(functools.partial(tell, barrier, "tp", tp_at(step)))

    for copy in small_copies[:4]:
        copy.wait()
    new_rows[...] = new_kv[...].astype(F32)
    slot_of = []
    for move in range(moves):
        rank = jnp.int32(0)
        for earlier in range(move):
            rank = rank + (migration[1, earlier] == migration[1, move]).astype(jnp.int32)
        slot_of.append((migration[1, move] - 1) * MIG_CAP + rank)
    page_pos = lax.broadcasted_iota(jnp.int32, (page_len, width), 0)

    for copy in pool_copies:
        copy.wait()
    weight_copy.start()

    def send_pages():
        pl.semaphore_wait(barrier, 2 * my_y + 1 - far + my_tp)
        for step in range(1, ROW):
            pl.when(my_y >= step)(
                functools.partial(tell, ready.at[0], "req", req_at(-step))
            )
        for step in range(1, n_tp):
            pl.when(my_tp >= step)(
                functools.partial(tell, ready.at[1], "tp", tp_at(-step))
            )
        first = MIG_CAP * (ROW - 1 - my_y)
        for turn in range(SLOTS):
            if turn in range(MIG_CAP, SLOTS, MIG_CAP):
                inner = turn // MIG_CAP - 1
                pl.when(my_y == inner)(
                    functools.partial(pl.semaphore_wait, ready.at[0], ROW - 1 - inner)
                )
            slot = lax.rem(first + turn, SLOTS)
            offset = lax.div(slot, MIG_CAP) + 1
            request, present = jnp.int32(0), jnp.int32(0)
            for move in range(moves):
                here = slot_of[move] == slot
                request = jnp.where(here, migration[0, move], request)
                present = jnp.where(here, 1, present)
            length = jnp.where(present == 1, cont_len[request], -1)
            new_row = new_rows[pl.ds(request, 1), :]
            relayed = far if turn // MIG_CAP == 1 else 0
            target = lax.rem(my_req + n_req + offset - ROW * relayed, n_req)
            place = slot + (SLOTS - MIG_CAP) * relayed
            for page in range(cont_pages):
                held = pool[cont_table[page, request]].astype(F32)
                pos = page_pos + page * page_len
                kept = jnp.where(pos < length, held, 0.0)
                kept = jnp.where(pos == length, new_row, kept)
                span = pl.ds(page * page_len, page_len)
                outgoing[slot, span, :] = kept.astype(BF16)
                pltpu.make_async_remote_copy(
                    src_ref=outgoing.at[slot, span],
                    dst_ref=arrived.at[place, span],
                    send_sem=mig_send.at[slot],
                    recv_sem=mig_recv.at[slot + relayed * (SLOTS - 2 * MIG_CAP + slot + page)],
                    device_id={"req": target},
                    device_id_type=MESH,
                ).start()

    def attend():
        for copy in small_copies[4:]:
            copy.wait()
        tile_pages = 8
        tile = tile_pages * page_len
        group_tiles = group_pages // tile_pages
        cont_rows = tile_pages // cont_pages
        row = lax.broadcasted_iota(jnp.int32, (rows, tile), 0)
        lane = lax.broadcasted_iota(jnp.int32, (rows, tile), 1)
        group_row = jnp.zeros((rows, tile), jnp.int32)
        length_row = jnp.zeros((rows, tile), jnp.int32)
        for request in range(rows):
            group_row = jnp.where(row == request, req_group[request], group_row)
            length_row = jnp.where(row == request, cont_len[request], length_row)

        tiles = []
        for group in range(groups):
            limit = jnp.where(group_row == group, prompt_len[group], 0)
            for part_of in range(group_tiles):
                names = [prompt_table[group, part_of * tile_pages + j] for j in range(tile_pages)]
                tiles.append((names, lane + part_of * tile < limit))
        cont_span = cont_pages * page_len
        for first in range(0, rows, cont_rows):
            names = [
                cont_table[j % cont_pages, first + j // cont_pages] for j in range(tile_pages)
            ]
            start = (row - first) * cont_span
            tiles.append((names, (lane >= start) & (lane < start + length_row)))

        scale = key_width ** (-0.5)
        queries = [query[:, twin * key_width : (twin + 1) * key_width] for twin in range(2)]
        contract_last = (((1,), (1,)), ((), ()))

        def scores(keys, mask, twin):
            product = lax.dot_general(
                queries[twin], keys, contract_last, preferred_element_type=F32
            )
            return jnp.where(mask, product * scale, NEG)

        score_tiles = []
        for names, mask in tiles:
            pair = []
            for twin in range(2):
                cols = slice(twin * key_width, (twin + 1) * key_width)
                keys = jnp.concatenate([pool[name, :, cols] for name in names], axis=0)
                pair.append(scores(keys, mask, twin))
            score_tiles.append(jnp.concatenate(pair, axis=0))
        own = lax.broadcasted_iota(jnp.int32, (rows, rows), 0) == lax.broadcasted_iota(
            jnp.int32, (rows, rows), 1
        )
        new_score = jnp.concatenate(
            [
                scores(new_kv[:, twin * key_width : (twin + 1) * key_width], own, twin)
                for twin in range(2)
            ],
            axis=0,
        )
        peak = functools.reduce(jnp.maximum, score_tiles)
        top = jnp.maximum(
            jnp.max(peak, axis=1, keepdims=True), jnp.max(new_score, axis=1, keepdims=True)
        )
        exp_tiles = [jnp.exp(score - top) for score in score_tiles]
        new_exp = jnp.exp(new_score - top)
        denominator = jnp.sum(sum(exp_tiles), axis=1, keepdims=True) + jnp.sum(
            new_exp, axis=1, keepdims=True
        )
        inverse = 1.0 / denominator
        mixture = jnp.dot(
            (new_exp * inverse).astype(BF16), new_kv[:, value_col:], preferred_element_type=F32
        )
        for (names, _), exp_tile in zip(tiles, exp_tiles):
            values = jnp.concatenate([pool[name, :, value_col:] for name in names], axis=0)
            mixture = mixture + jnp.dot(
                (exp_tile * inverse).astype(BF16), values, preferred_element_type=F32
            )
        difference = mixture[:rows] - diff_lambda[0] * mixture[rows:]
        square = jnp.mean(difference * difference, axis=1, keepdims=True)
        mixed[...] = (difference * lax.rsqrt(square + 1e-05) * 0.8).astype(BF16)


    send_pages()
    attend()

    def relay(slot, page):
        span = pl.ds(page * page_len, page_len)
        return pltpu.make_async_remote_copy(
            src_ref=arrived.at[SLOTS + slot, span],
            dst_ref=arrived.at[MIG_CAP + slot, span],
            send_sem=mig_send.at[SLOTS + slot],
            recv_sem=mig_recv.at[MIG_CAP + slot],
            device_id={"req": lax.rem(my_req + ROW, n_req)},
            device_id_type=MESH,
        )

    def wait_bytes(ref, sem):
        pltpu.make_async_copy(ref, ref, sem).wait()

    def pass_on():
        for slot in range(MIG_CAP):
            for page in range(cont_pages):
                span = pl.ds(page * page_len, page_len)
                wait_bytes(
                    arrived.at[SLOTS + slot, span], mig_recv.at[SLOTS + 2 * slot + page]
                )
                relay(slot, page).start()

    attention = mixed[...]
    weight_copy.wait()

    def columns(index):
        return pl.ds(pl.multiple_of(index * block, block), block)


    @pl.when(my_tp < n_tp - 1)
    def _():
        pl.semaphore_wait(ready.at[1], n_tp - 1 - my_tp)

    sum_copies = []
    for step in (4, 3, 5, 2, 6, 1, 7):
        peer = lax.rem(my_tp + step, n_tp)
        part[step] = jnp.dot(
            attention, weight[:, columns(peer)], preferred_element_type=F32
        ).astype(BF16)
        copy = pltpu.make_async_remote_copy(
            src_ref=part.at[step],
            dst_ref=sum_in.at[step],
            send_sem=sum_send.at[step],
            recv_sem=sum_recv.at[step],
            device_id={"tp": peer},
            device_id_type=MESH,
        )
        copy.start()
        sum_copies.append((step, copy))
    pl.when(my_y == 1)(pass_on)
    own_part = jnp.dot(
        attention, weight[:, columns(my_tp)], preferred_element_type=F32
    )
    summed = hidden_in[:, columns(my_tp)].astype(F32) + own_part
    for step, copy in reversed(sum_copies):
        copy.wait_recv()
        summed = summed + sum_in[step].astype(F32)
    total[my_tp] = summed.astype(BF16)
    all_copies = []
    for step in (4, 3, 5, 2, 6, 1, 7):
        peer = lax.rem(my_tp + step, n_tp)
        copy = pltpu.make_async_remote_copy(
            src_ref=total.at[my_tp],
            dst_ref=total.at[my_tp],
            send_sem=all_send.at[step],
            recv_sem=all_recv.at[step],
            device_id={"tp": peer},
            device_id_type=MESH,
        )
        copy.start()
        all_copies.append(copy)
    for copy in reversed(all_copies):
        copy.wait_recv()
    blocks = [total[index].astype(F32) for index in range(n_tp)]
    square_sum = functools.reduce(jnp.add, [value * value for value in blocks])
    mean = jnp.sum(square_sum, axis=1, keepdims=True) / (block * n_tp)
    factor = lax.rsqrt(mean + 1e-05)
    for index, value in enumerate(blocks):
        cols = slice(index * block, (index + 1) * block)
        hidden_out[:, cols] = value.astype(BF16)
        normed_out[:, cols] = (value * factor * norm_gain[:, cols]).astype(BF16)
    for _, copy in sum_copies:
        copy.wait_send()
    for copy in all_copies:
        copy.wait_send()
    for slot in range(SLOTS):
        wait_bytes(outgoing.at[slot], mig_send.at[slot])
        wait_bytes(arrived.at[slot], mig_recv.at[slot])

    @pl.when(my_y == 1)
    def _():
        for slot in range(MIG_CAP):
            wait_bytes(arrived.at[SLOTS + slot], mig_send.at[SLOTS + slot])


def store_kernel(*refs):
    count = len(refs) // 2
    copies = [
        pltpu.make_async_copy(
            refs[index].at[pl.ds(0, refs[count + index].shape[0])],
            refs[count + index],
            refs[-1].at[index],
        )
        for index in range(count)
    ]
    for copy in copies:
        copy.start()
    for copy in copies:
        copy.wait()


def shards(
    n_req,
    n_tp,
    hidden_in,
    query,
    new_kv,
    pool_cache,
    prompt_table,
    prompt_len,
    req_group,
    cont_table,
    cont_len,
    migration,
    diff_lambda,
    out_weight,
    norm_gain,
):
    rows, model = hidden_in.shape
    pages, page_len, width = pool_cache.shape
    span = cont_table.shape[1] * page_len
    block = model // n_tp
    operands = (
        prompt_table,
        prompt_len,
        req_group,
        cont_table.T,
        cont_len,
        migration.T,
        diff_lambda,
        hidden_in,
        query,
        new_kv,
        norm_gain.reshape(1, model),
        pool_cache,
        out_weight,
    )
    anywhere = pl.BlockSpec(memory_space=pl.ANY)
    vmem = pl.BlockSpec(memory_space=pltpu.VMEM)
    shapes = ((rows, model), (rows, model), (SLOTS, span, width))
    landing = ((rows, model), (rows, model), (SLOTS + RELAYS, span, width))
    results = pl.pallas_call(
        functools.partial(layer_kernel, n_req, n_tp),
        out_shape=tuple(pltpu.VMEM(shape, BF16) for shape in landing),
        in_specs=[anywhere] * len(operands),
        out_specs=(vmem,) * len(shapes),
        scratch_shapes=[
            *(pltpu.SMEM(value.shape, value.dtype) for value in operands[:7]),
            *(pltpu.VMEM(value.shape, value.dtype) for value in operands[7:]),
            pltpu.VMEM((rows, width), F32),
            pltpu.VMEM((rows, out_weight.shape[0]), BF16),
            pltpu.VMEM((SLOTS, span, width), BF16),
            pltpu.VMEM((n_tp, rows, block), BF16),
            pltpu.VMEM((n_tp, rows, block), BF16),
            pltpu.VMEM((n_tp, rows, block), BF16),
            pltpu.SemaphoreType.REGULAR((2,)),
            pltpu.SemaphoreType.DMA((11,)),
            pltpu.SemaphoreType.DMA((POOL_CHUNKS,)),
            pltpu.SemaphoreType.DMA,
            pltpu.SemaphoreType.DMA((SLOTS + RELAYS,)),
            pltpu.SemaphoreType.DMA((SLOTS + RELAYS * CONT_PAGES,)),
            pltpu.SemaphoreType.DMA((n_tp,)),
            pltpu.SemaphoreType.DMA((n_tp,)),
            pltpu.SemaphoreType.DMA((n_tp,)),
            pltpu.SemaphoreType.DMA((n_tp,)),
        ],
        compiler_params=pltpu.CompilerParams(collective_id=0, has_side_effects=True),
        name="decode_layer",
    )(*operands)
    return pl.pallas_call(
        store_kernel,
        out_shape=tuple(jax.ShapeDtypeStruct(shape, BF16) for shape in shapes),
        in_specs=[vmem] * len(shapes),
        out_specs=(anywhere,) * len(shapes),
        scratch_shapes=[pltpu.SemaphoreType.DMA((len(shapes),))],
        name="store_results",
    )(*(pltpu.with_memory_space_constraint(value, pltpu.VMEM) for value in results))


def solution(mesh):
    placed = (
        P("req", None),
        P("req", "tp"),
        P("req", "tp"),
        P("req", None, "tp"),
        P("req", None),
        P("req"),
        P("req"),
        P("req", None),
        P("req"),
        P("req", None),
        P("tp"),
        P("tp", None),
        P(),
    )
    return jax.shard_map(
        functools.partial(shards, mesh.shape["req"], mesh.shape["tp"]),
        mesh=mesh,
        in_specs=placed,
        out_specs=(P("req", None), P("req", None), P("req", None, "tp")),
        check_vma=False,
    )
```

```python
import functools

import jax
import jax.numpy as jnp
from jax import lax
from jax.experimental import pallas as pl
from jax.experimental.pallas import tpu as pltpu
from jax.sharding import PartitionSpec as P

MIG_REACH = 4
MIG_CAP = 2
SLOTS = MIG_REACH * MIG_CAP
RELAYS = MIG_CAP
ROW = 4
CONT_PAGES = 2
POOL_CHUNKS = 2
MESH = pl.DeviceIdType.MESH
F32 = jnp.float32
BF16 = jnp.bfloat16
NEG = -1e30


def layer_kernel(
    n_req,
    n_tp,
    prompt_table_hbm,
    prompt_len_hbm,
    req_group_hbm,
    cont_table_hbm,
    cont_len_hbm,
    migration_hbm,
    diff_lambda_hbm,
    hidden_in_hbm,
    query_hbm,
    new_kv_hbm,
    norm_gain_hbm,
    pool_hbm,
    weight_hbm,
    hidden_out,
    normed_out,
    arrived,
    prompt_table,
    prompt_len,
    req_group,
    cont_table,
    cont_len,
    migration,
    diff_lambda,
    hidden_in,
    query,
    new_kv,
    norm_gain,
    pool,
    weight,
    new_rows,
    mixed,
    outgoing,
    part,
    sum_in,
    total,
    ready,
    small_sem,
    pool_sem,
    weight_sem,
    mig_send,
    mig_recv,
    sum_send,
    sum_recv,
    all_send,
    all_recv,
):
    rows, key_width = query.shape[0], query.shape[1] // 2
    pages, page_len, width = pool.shape
    value_col = 2 * key_width
    groups, group_pages = prompt_table.shape
    cont_pages = cont_table.shape[0]
    moves = migration.shape[1]
    block = total.shape[2]
    my_req = lax.axis_index("req")
    my_tp = lax.axis_index("tp")

    tables = (
        (migration_hbm, migration),
        (cont_table_hbm, cont_table),
        (cont_len_hbm, cont_len),
        (new_kv_hbm, new_kv),
        (prompt_table_hbm, prompt_table),
        (prompt_len_hbm, prompt_len),
        (req_group_hbm, req_group),
        (diff_lambda_hbm, diff_lambda),
        (query_hbm, query),
        (hidden_in_hbm, hidden_in),
        (norm_gain_hbm, norm_gain),
    )
    small_copies = [
        pltpu.make_async_copy(source, target, small_sem.at[index])
        for index, (source, target) in enumerate(tables)
    ]
    per_chunk = pages // POOL_CHUNKS
    pool_copies = []
    for chunk in range(POOL_CHUNKS):
        piece = pl.ds(chunk * per_chunk, per_chunk)
        pool_copies.append(
            pltpu.make_async_copy(pool_hbm.at[piece], pool.at[piece], pool_sem.at[chunk])
        )
        pool_copies[-1].start()
    weight_copy = pltpu.make_async_copy(weight_hbm, weight, weight_sem)
    for copy in small_copies:
        copy.start()

    barrier = pltpu.get_barrier_semaphore()
    my_y = lax.rem(my_req, ROW)
    far = (my_y == ROW - 1).astype(jnp.int32)

    def tell(semaphore, axis, index):
        pl.semaphore_signal(
            semaphore, inc=1, device_id={axis: index}, device_id_type=MESH
        )

    def req_at(step):
        return lax.rem(my_req + n_req + step, n_req)

    def swapped(index):
        return index + 1 - 2 * lax.rem(index, 2)

    turn_of = swapped(my_tp)

    def tp_at(step):
        return swapped(lax.rem(turn_of + n_tp + step, n_tp))

    for offset in range(1, MIG_REACH + 1):
        crosses = my_y < offset
        if offset == 2:
            crosses = crosses & (my_y != 1)
        pl.when(crosses)(functools.partial(tell, barrier, "req", req_at(-offset)))
    for step in range(1, ROW):
        pl.when(my_y + step < ROW)(functools.partial(tell, barrier, "req", req_at(step)))
    for step in range(1, n_tp):
        pl.when(turn_of + step < n_tp)(functools.partial(tell, barrier, "tp", tp_at(step)))

    for copy in small_copies[:4]:
        copy.wait()
    new_rows[...] = new_kv[...].astype(F32)
    slot_of = []
    for move in range(moves):
        rank = jnp.int32(0)
        for earlier in range(move):
            rank = rank + (migration[1, earlier] == migration[1, move]).astype(jnp.int32)
        slot_of.append((migration[1, move] - 1) * MIG_CAP + rank)
    page_pos = lax.broadcasted_iota(jnp.int32, (page_len, width), 0)

    for copy in pool_copies:
        copy.wait()
    weight_copy.start()

    def send_pages():
        pl.semaphore_wait(barrier, 2 * my_y + 1 - far + turn_of)
        for step in range(1, ROW):
            pl.when(my_y >= step)(
                functools.partial(tell, ready.at[0], "req", req_at(-step))
            )
        for step in range(1, n_tp):
            pl.when(turn_of >= step)(
                functools.partial(tell, ready.at[1], "tp", tp_at(-step))
            )
        first = MIG_CAP * (ROW - 1 - my_y)
        for turn in range(SLOTS):
            if turn in range(MIG_CAP, SLOTS, MIG_CAP):
                inner = turn // MIG_CAP - 1
                pl.when(my_y == inner)(
                    functools.partial(pl.semaphore_wait, ready.at[0], ROW - 1 - inner)
                )
            slot = lax.rem(first + turn, SLOTS)
            offset = lax.div(slot, MIG_CAP) + 1
            request, present = jnp.int32(0), jnp.int32(0)
            for move in range(moves):
                here = slot_of[move] == slot
                request = jnp.where(here, migration[0, move], request)
                present = jnp.where(here, 1, present)
            length = jnp.where(present == 1, cont_len[request], -1)
            new_row = new_rows[pl.ds(request, 1), :]
            relayed = far if turn // MIG_CAP == 1 else 0
            target = lax.rem(my_req + n_req + offset - ROW * relayed, n_req)
            place = slot + (SLOTS - MIG_CAP) * relayed
            for page in range(cont_pages):
                held = pool[cont_table[page, request]].astype(F32)
                pos = page_pos + page * page_len
                kept = jnp.where(pos < length, held, 0.0)
                kept = jnp.where(pos == length, new_row, kept)
                span = pl.ds(page * page_len, page_len)
                outgoing[slot, span, :] = kept.astype(BF16)
                pltpu.make_async_remote_copy(
                    src_ref=outgoing.at[slot, span],
                    dst_ref=arrived.at[place, span],
                    send_sem=mig_send.at[slot],
                    recv_sem=mig_recv.at[slot + relayed * (SLOTS - 2 * MIG_CAP + slot + page)],
                    device_id={"req": target},
                    device_id_type=MESH,
                ).start()

    def attend():
        for copy in small_copies[4:]:
            copy.wait()
        tile_pages = 8
        tile = tile_pages * page_len
        group_tiles = group_pages // tile_pages
        cont_rows = tile_pages // cont_pages
        row = lax.broadcasted_iota(jnp.int32, (rows, tile), 0)
        lane = lax.broadcasted_iota(jnp.int32, (rows, tile), 1)
        group_row = jnp.zeros((rows, tile), jnp.int32)
        length_row = jnp.zeros((rows, tile), jnp.int32)
        for request in range(rows):
            group_row = jnp.where(row == request, req_group[request], group_row)
            length_row = jnp.where(row == request, cont_len[request], length_row)

        tiles = []
        for group in range(groups):
            limit = jnp.where(group_row == group, prompt_len[group], 0)
            for part_of in range(group_tiles):
                names = [prompt_table[group, part_of * tile_pages + j] for j in range(tile_pages)]
                tiles.append((names, lane + part_of * tile < limit))
        cont_span = cont_pages * page_len
        for first in range(0, rows, cont_rows):
            names = [
                cont_table[j % cont_pages, first + j // cont_pages] for j in range(tile_pages)
            ]
            start = (row - first) * cont_span
            tiles.append((names, (lane >= start) & (lane < start + length_row)))

        scale = key_width ** (-0.5)
        queries = [query[:, twin * key_width : (twin + 1) * key_width] for twin in range(2)]
        contract_last = (((1,), (1,)), ((), ()))

        def scores(keys, mask, twin):
            product = lax.dot_general(
                queries[twin], keys, contract_last, preferred_element_type=F32
            )
            return jnp.where(mask, product * scale, NEG)

        score_tiles = []
        for names, mask in tiles:
            pair = []
            for twin in range(2):
                cols = slice(twin * key_width, (twin + 1) * key_width)
                keys = jnp.concatenate([pool[name, :, cols] for name in names], axis=0)
                pair.append(scores(keys, mask, twin))
            score_tiles.append(jnp.concatenate(pair, axis=0))
        own = lax.broadcasted_iota(jnp.int32, (rows, rows), 0) == lax.broadcasted_iota(
            jnp.int32, (rows, rows), 1
        )
        new_score = jnp.concatenate(
            [
                scores(new_kv[:, twin * key_width : (twin + 1) * key_width], own, twin)
                for twin in range(2)
            ],
            axis=0,
        )
        peak = functools.reduce(jnp.maximum, score_tiles)
        top = jnp.maximum(
            jnp.max(peak, axis=1, keepdims=True), jnp.max(new_score, axis=1, keepdims=True)
        )
        exp_tiles = [jnp.exp(score - top) for score in score_tiles]
        new_exp = jnp.exp(new_score - top)
        denominator = jnp.sum(sum(exp_tiles), axis=1, keepdims=True) + jnp.sum(
            new_exp, axis=1, keepdims=True
        )
        inverse = 1.0 / denominator
        mixture = jnp.dot(
            (new_exp * inverse).astype(BF16), new_kv[:, value_col:], preferred_element_type=F32
        )
        for (names, _), exp_tile in zip(tiles, exp_tiles):
            values = jnp.concatenate([pool[name, :, value_col:] for name in names], axis=0)
            mixture = mixture + jnp.dot(
                (exp_tile * inverse).astype(BF16), values, preferred_element_type=F32
            )
        difference = mixture[:rows] - diff_lambda[0] * mixture[rows:]
        square = jnp.mean(difference * difference, axis=1, keepdims=True)
        mixed[...] = (difference * lax.rsqrt(square + 1e-05) * 0.8).astype(BF16)


    send_pages()
    attend()

    def relay(slot, page):
        span = pl.ds(page * page_len, page_len)
        return pltpu.make_async_remote_copy(
            src_ref=arrived.at[SLOTS + slot, span],
            dst_ref=arrived.at[MIG_CAP + slot, span],
            send_sem=mig_send.at[SLOTS + slot],
            recv_sem=mig_recv.at[MIG_CAP + slot],
            device_id={"req": lax.rem(my_req + ROW, n_req)},
            device_id_type=MESH,
        )

    def wait_bytes(ref, sem):
        pltpu.make_async_copy(ref, ref, sem).wait()

    def pass_on():
        for slot in range(MIG_CAP):
            for page in range(cont_pages):
                span = pl.ds(page * page_len, page_len)
                wait_bytes(
                    arrived.at[SLOTS + slot, span], mig_recv.at[SLOTS + 2 * slot + page]
                )
                relay(slot, page).start()

    attention = mixed[...]
    weight_copy.wait()

    def columns(index):
        return pl.ds(pl.multiple_of(index * block, block), block)


    @pl.when(turn_of < n_tp - 1)
    def _():
        pl.semaphore_wait(ready.at[1], n_tp - 1 - turn_of)

    sum_copies = []
    for step in (4, 3, 5, 2, 6, 1, 7):
        peer = lax.rem(my_tp + step, n_tp)
        part[step] = jnp.dot(
            attention, weight[:, columns(peer)], preferred_element_type=F32
        ).astype(BF16)
        copy = pltpu.make_async_remote_copy(
            src_ref=part.at[step],
            dst_ref=sum_in.at[step],
            send_sem=sum_send.at[step],
            recv_sem=sum_recv.at[step],
            device_id={"tp": peer},
            device_id_type=MESH,
        )
        copy.start()
        sum_copies.append((step, copy))
    pl.when(my_y == 1)(pass_on)
    own_part = jnp.dot(
        attention, weight[:, columns(my_tp)], preferred_element_type=F32
    )
    summed = hidden_in[:, columns(my_tp)].astype(F32) + own_part
    for step, copy in reversed(sum_copies):
        copy.wait_recv()
        summed = summed + sum_in[step].astype(F32)
    total[my_tp] = summed.astype(BF16)
    all_copies = []
    for step in (4, 3, 5, 2, 6, 1, 7):
        peer = lax.rem(my_tp + step, n_tp)
        copy = pltpu.make_async_remote_copy(
            src_ref=total.at[my_tp],
            dst_ref=total.at[my_tp],
            send_sem=all_send.at[step],
            recv_sem=all_recv.at[step],
            device_id={"tp": peer},
            device_id_type=MESH,
        )
        copy.start()
        all_copies.append(copy)
    for copy in reversed(all_copies):
        copy.wait_recv()
    blocks = [total[index].astype(F32) for index in range(n_tp)]
    square_sum = functools.reduce(jnp.add, [value * value for value in blocks])
    mean = jnp.sum(square_sum, axis=1, keepdims=True) / (block * n_tp)
    factor = lax.rsqrt(mean + 1e-05)
    for index, value in enumerate(blocks):
        cols = slice(index * block, (index + 1) * block)
        hidden_out[:, cols] = value.astype(BF16)
        normed_out[:, cols] = (value * factor * norm_gain[:, cols]).astype(BF16)
    for _, copy in sum_copies:
        copy.wait_send()
    for copy in all_copies:
        copy.wait_send()
    for slot in range(SLOTS):
        wait_bytes(outgoing.at[slot], mig_send.at[slot])
        wait_bytes(arrived.at[slot], mig_recv.at[slot])

    @pl.when(my_y == 1)
    def _():
        for slot in range(MIG_CAP):
            wait_bytes(arrived.at[SLOTS + slot], mig_send.at[SLOTS + slot])


def store_kernel(*refs):
    count = len(refs) // 2
    copies = [
        pltpu.make_async_copy(
            refs[index].at[pl.ds(start, step)],
            refs[count + index].at[pl.ds(start, step)],
            refs[-1].at[index],
        )
        for index in range(count)
        for step in [refs[count + index].shape[0] // (4 if index == count - 1 else 1)]
        for start in range(0, refs[count + index].shape[0], step)
    ]
    for copy in copies:
        copy.start()
    for copy in copies:
        copy.wait()


def shards(
    n_req,
    n_tp,
    hidden_in,
    query,
    new_kv,
    pool_cache,
    prompt_table,
    prompt_len,
    req_group,
    cont_table,
    cont_len,
    migration,
    diff_lambda,
    out_weight,
    norm_gain,
):
    rows, model = hidden_in.shape
    pages, page_len, width = pool_cache.shape
    span = cont_table.shape[1] * page_len
    block = model // n_tp
    operands = (
        prompt_table,
        prompt_len,
        req_group,
        cont_table.T,
        cont_len,
        migration.T,
        diff_lambda,
        hidden_in,
        query,
        new_kv,
        norm_gain.reshape(1, model),
        pool_cache,
        out_weight,
    )
    anywhere = pl.BlockSpec(memory_space=pl.ANY)
    vmem = pl.BlockSpec(memory_space=pltpu.VMEM)
    shapes = ((rows, model), (rows, model), (SLOTS, span, width))
    landing = ((rows, model), (rows, model), (SLOTS + RELAYS, span, width))
    results = pl.pallas_call(
        functools.partial(layer_kernel, n_req, n_tp),
        out_shape=tuple(pltpu.VMEM(shape, BF16) for shape in landing),
        in_specs=[anywhere] * len(operands),
        out_specs=(vmem,) * len(shapes),
        scratch_shapes=[
            *(pltpu.SMEM(value.shape, value.dtype) for value in operands[:7]),
            *(pltpu.VMEM(value.shape, value.dtype) for value in operands[7:]),
            pltpu.VMEM((rows, width), F32),
            pltpu.VMEM((rows, out_weight.shape[0]), BF16),
            pltpu.VMEM((SLOTS, span, width), BF16),
            pltpu.VMEM((n_tp, rows, block), BF16),
            pltpu.VMEM((n_tp, rows, block), BF16),
            pltpu.VMEM((n_tp, rows, block), BF16),
            pltpu.SemaphoreType.REGULAR((2,)),
            pltpu.SemaphoreType.DMA((11,)),
            pltpu.SemaphoreType.DMA((POOL_CHUNKS,)),
            pltpu.SemaphoreType.DMA,
            pltpu.SemaphoreType.DMA((SLOTS + RELAYS,)),
            pltpu.SemaphoreType.DMA((SLOTS + RELAYS * CONT_PAGES,)),
            pltpu.SemaphoreType.DMA((n_tp,)),
            pltpu.SemaphoreType.DMA((n_tp,)),
            pltpu.SemaphoreType.DMA((n_tp,)),
            pltpu.SemaphoreType.DMA((n_tp,)),
        ],
        compiler_params=pltpu.CompilerParams(collective_id=0, has_side_effects=True),
        name="decode_layer",
    )(*operands)
    return pl.pallas_call(
        store_kernel,
        out_shape=tuple(jax.ShapeDtypeStruct(shape, BF16) for shape in shapes),
        in_specs=[vmem] * len(shapes),
        out_specs=(anywhere,) * len(shapes),
        scratch_shapes=[pltpu.SemaphoreType.DMA((len(shapes),))],
        name="store_results",
    )(*(pltpu.with_memory_space_constraint(value, pltpu.VMEM) for value in results))


def solution(mesh):
    placed = (
        P("req", None),
        P("req", "tp"),
        P("req", "tp"),
        P("req", None, "tp"),
        P("req", None),
        P("req"),
        P("req"),
        P("req", None),
        P("req"),
        P("req", None),
        P("tp"),
        P("tp", None),
        P(),
    )
    return jax.shard_map(
        functools.partial(shards, mesh.shape["req"], mesh.shape["tp"]),
        mesh=mesh,
        in_specs=placed,
        out_specs=(P("req", None), P("req", None), P("req", None, "tp")),
        check_vma=False,
    )
```

```python
import functools

import jax
import jax.numpy as jnp
from jax import lax
from jax.experimental import pallas as pl
from jax.experimental.pallas import tpu as pltpu
from jax.sharding import PartitionSpec as P

MIG_REACH = 4
MIG_CAP = 2
SLOTS = MIG_REACH * MIG_CAP
RELAYS = MIG_CAP
ROW = 4
CONT_PAGES = 2
POOL_CHUNKS = 1
MESH = pl.DeviceIdType.MESH
F32 = jnp.float32
BF16 = jnp.bfloat16
NEG = -1e30


def layer_kernel(
    n_req,
    n_tp,
    prompt_table_hbm,
    prompt_len_hbm,
    req_group_hbm,
    cont_table_hbm,
    cont_len_hbm,
    migration_hbm,
    diff_lambda_hbm,
    hidden_in_hbm,
    query_hbm,
    new_kv_hbm,
    norm_gain_hbm,
    pool_hbm,
    weight_hbm,
    hidden_out,
    normed_out,
    arrived,
    prompt_table,
    prompt_len,
    req_group,
    cont_table,
    cont_len,
    migration,
    diff_lambda,
    hidden_in,
    query,
    new_kv,
    norm_gain,
    pool,
    weight,
    new_rows,
    mixed,
    outgoing,
    part,
    sum_in,
    total,
    ready,
    small_sem,
    pool_sem,
    weight_sem,
    mig_send,
    mig_recv,
    sum_send,
    sum_recv,
    all_send,
    all_recv,
):
    rows, key_width = query.shape[0], query.shape[1] // 2
    pages, page_len, width = pool.shape
    value_col = 2 * key_width
    groups, group_pages = prompt_table.shape
    cont_pages = cont_table.shape[0]
    moves = migration.shape[1]
    block = total.shape[2]
    my_req = lax.axis_index("req")
    my_tp = lax.axis_index("tp")

    tables = (
        (migration_hbm, migration),
        (cont_table_hbm, cont_table),
        (cont_len_hbm, cont_len),
        (new_kv_hbm, new_kv),
        (prompt_table_hbm, prompt_table),
        (prompt_len_hbm, prompt_len),
        (req_group_hbm, req_group),
        (diff_lambda_hbm, diff_lambda),
        (query_hbm, query),
        (hidden_in_hbm, hidden_in),
        (norm_gain_hbm, norm_gain),
    )
    small_copies = [
        pltpu.make_async_copy(source, target, small_sem.at[index])
        for index, (source, target) in enumerate(tables)
    ]
    per_chunk = pages // POOL_CHUNKS
    pool_copies = []
    for chunk in range(POOL_CHUNKS):
        piece = pl.ds(chunk * per_chunk, per_chunk)
        pool_copies.append(
            pltpu.make_async_copy(pool_hbm.at[piece], pool.at[piece], pool_sem.at[chunk])
        )
        pool_copies[-1].start()
    weight_copy = pltpu.make_async_copy(weight_hbm, weight, weight_sem)
    for copy in small_copies:
        copy.start()

    barrier = pltpu.get_barrier_semaphore()
    my_y = lax.rem(my_req, ROW)
    far = (my_y == ROW - 1).astype(jnp.int32)

    def tell(semaphore, axis, index):
        pl.semaphore_signal(
            semaphore, inc=1, device_id={axis: index}, device_id_type=MESH
        )

    def req_at(step):
        return lax.rem(my_req + n_req + step, n_req)

    def swapped(index):
        return index + 1 - 2 * lax.rem(index, 2)

    turn_of = swapped(my_tp)

    def tp_at(step):
        return swapped(lax.rem(turn_of + n_tp + step, n_tp))

    for offset in range(1, MIG_REACH + 1):
        crosses = my_y < offset
        if offset == 2:
            crosses = crosses & (my_y != 1)
        pl.when(crosses)(functools.partial(tell, barrier, "req", req_at(-offset)))
    for step in range(1, ROW):
        pl.when(my_y + step < ROW)(functools.partial(tell, barrier, "req", req_at(step)))
    for step in range(1, n_tp):
        pl.when(turn_of + step < n_tp)(functools.partial(tell, barrier, "tp", tp_at(step)))

    for copy in small_copies[:4]:
        copy.wait()
    new_rows[...] = new_kv[...].astype(F32)
    slot_of = []
    for move in range(moves):
        rank = jnp.int32(0)
        for earlier in range(move):
            rank = rank + (migration[1, earlier] == migration[1, move]).astype(jnp.int32)
        slot_of.append((migration[1, move] - 1) * MIG_CAP + rank)
    page_pos = lax.broadcasted_iota(jnp.int32, (page_len, width), 0)

    for copy in pool_copies:
        copy.wait()
    weight_copy.start()

    def send_pages():
        pl.semaphore_wait(barrier, 2 * my_y + 1 - far + turn_of)
        for step in range(1, ROW):
            pl.when(my_y >= step)(
                functools.partial(tell, ready.at[0], "req", req_at(-step))
            )
        for step in range(1, n_tp):
            pl.when(turn_of >= step)(
                functools.partial(tell, ready.at[1], "tp", tp_at(-step))
            )
        first = MIG_CAP * (ROW - 1 - my_y)
        for turn in range(SLOTS):
            if turn in range(MIG_CAP, SLOTS, MIG_CAP):
                inner = turn // MIG_CAP - 1
                pl.when(my_y == inner)(
                    functools.partial(pl.semaphore_wait, ready.at[0], ROW - 1 - inner)
                )
            slot = lax.rem(first + turn, SLOTS)
            offset = lax.div(slot, MIG_CAP) + 1
            request, present = jnp.int32(0), jnp.int32(0)
            for move in range(moves):
                here = slot_of[move] == slot
                request = jnp.where(here, migration[0, move], request)
                present = jnp.where(here, 1, present)
            length = jnp.where(present == 1, cont_len[request], -1)
            new_row = new_rows[pl.ds(request, 1), :]
            relayed = far if turn // MIG_CAP == 1 else 0
            target = lax.rem(my_req + n_req + offset - ROW * relayed, n_req)
            place = slot + (SLOTS - MIG_CAP) * relayed
            for page in range(cont_pages):
                held = pool[cont_table[page, request]].astype(F32)
                pos = page_pos + page * page_len
                kept = jnp.where(pos < length, held, 0.0)
                kept = jnp.where(pos == length, new_row, kept)
                span = pl.ds(page * page_len, page_len)
                outgoing[slot, span, :] = kept.astype(BF16)
                pltpu.make_async_remote_copy(
                    src_ref=outgoing.at[slot, span],
                    dst_ref=arrived.at[place, span],
                    send_sem=mig_send.at[slot],
                    recv_sem=mig_recv.at[slot + relayed * (SLOTS - 2 * MIG_CAP + slot + page)],
                    device_id={"req": target},
                    device_id_type=MESH,
                ).start()

    def attend():
        for copy in small_copies[4:]:
            copy.wait()
        tile_pages = 8
        tile = tile_pages * page_len
        group_tiles = group_pages // tile_pages
        cont_rows = tile_pages // cont_pages
        row = lax.broadcasted_iota(jnp.int32, (rows, tile), 0)
        lane = lax.broadcasted_iota(jnp.int32, (rows, tile), 1)
        group_row = jnp.zeros((rows, tile), jnp.int32)
        length_row = jnp.zeros((rows, tile), jnp.int32)
        for request in range(rows):
            group_row = jnp.where(row == request, req_group[request], group_row)
            length_row = jnp.where(row == request, cont_len[request], length_row)

        tiles = []
        for group in range(groups):
            limit = jnp.where(group_row == group, prompt_len[group], 0)
            for part_of in range(group_tiles):
                names = [prompt_table[group, part_of * tile_pages + j] for j in range(tile_pages)]
                tiles.append((names, lane + part_of * tile < limit))
        cont_span = cont_pages * page_len
        for first in range(0, rows, cont_rows):
            names = [
                cont_table[j % cont_pages, first + j // cont_pages] for j in range(tile_pages)
            ]
            start = (row - first) * cont_span
            tiles.append((names, (lane >= start) & (lane < start + length_row)))

        scale = key_width ** (-0.5)
        queries = [query[:, twin * key_width : (twin + 1) * key_width] for twin in range(2)]
        contract_last = (((1,), (1,)), ((), ()))

        def scores(keys, mask, twin):
            product = lax.dot_general(
                queries[twin], keys, contract_last, preferred_element_type=F32
            )
            return jnp.where(mask, product * scale, NEG)

        score_tiles = []
        for names, mask in tiles:
            pair = []
            for twin in range(2):
                cols = slice(twin * key_width, (twin + 1) * key_width)
                keys = jnp.concatenate([pool[name, :, cols] for name in names], axis=0)
                pair.append(scores(keys, mask, twin))
            score_tiles.append(jnp.concatenate(pair, axis=0))
        own = lax.broadcasted_iota(jnp.int32, (rows, rows), 0) == lax.broadcasted_iota(
            jnp.int32, (rows, rows), 1
        )
        new_score = jnp.concatenate(
            [
                scores(new_kv[:, twin * key_width : (twin + 1) * key_width], own, twin)
                for twin in range(2)
            ],
            axis=0,
        )
        peak = functools.reduce(jnp.maximum, score_tiles)
        top = jnp.maximum(
            jnp.max(peak, axis=1, keepdims=True), jnp.max(new_score, axis=1, keepdims=True)
        )
        exp_tiles = [jnp.exp(score - top) for score in score_tiles]
        new_exp = jnp.exp(new_score - top)
        denominator = jnp.sum(sum(exp_tiles), axis=1, keepdims=True) + jnp.sum(
            new_exp, axis=1, keepdims=True
        )
        inverse = 1.0 / denominator
        mixture = jnp.dot(
            (new_exp * inverse).astype(BF16), new_kv[:, value_col:], preferred_element_type=F32
        )
        for (names, _), exp_tile in zip(tiles, exp_tiles):
            values = jnp.concatenate([pool[name, :, value_col:] for name in names], axis=0)
            mixture = mixture + jnp.dot(
                (exp_tile * inverse).astype(BF16), values, preferred_element_type=F32
            )
        difference = mixture[:rows] - diff_lambda[0] * mixture[rows:]
        square = jnp.mean(difference * difference, axis=1, keepdims=True)
        mixed[...] = (difference * lax.rsqrt(square + 1e-05) * 0.8).astype(BF16)


    send_pages()
    attend()

    def relay(slot, page):
        span = pl.ds(page * page_len, page_len)
        return pltpu.make_async_remote_copy(
            src_ref=arrived.at[SLOTS + slot, span],
            dst_ref=arrived.at[MIG_CAP + slot, span],
            send_sem=mig_send.at[SLOTS + slot],
            recv_sem=mig_recv.at[MIG_CAP + slot],
            device_id={"req": lax.rem(my_req + ROW, n_req)},
            device_id_type=MESH,
        )

    def wait_bytes(ref, sem):
        pltpu.make_async_copy(ref, ref, sem).wait()

    def pass_on():
        for slot in range(MIG_CAP):
            for page in range(cont_pages):
                span = pl.ds(page * page_len, page_len)
                wait_bytes(
                    arrived.at[SLOTS + slot, span], mig_recv.at[SLOTS + 2 * slot + page]
                )
                relay(slot, page).start()

    attention = mixed[...]
    weight_copy.wait()

    def columns(index):
        return pl.ds(pl.multiple_of(index * block, block), block)


    @pl.when(turn_of < n_tp - 1)
    def _():
        pl.semaphore_wait(ready.at[1], n_tp - 1 - turn_of)

    sum_copies = []
    for step in (4, 3, 5, 2, 6, 1, 7):
        peer = lax.rem(my_tp + step, n_tp)
        part[step] = jnp.dot(
            attention, weight[:, columns(peer)], preferred_element_type=F32
        ).astype(BF16)
        copy = pltpu.make_async_remote_copy(
            src_ref=part.at[step],
            dst_ref=sum_in.at[step],
            send_sem=sum_send.at[step],
            recv_sem=sum_recv.at[step],
            device_id={"tp": peer},
            device_id_type=MESH,
        )
        copy.start()
        sum_copies.append((step, copy))
    pl.when(my_y == 1)(pass_on)
    own_part = jnp.dot(
        attention, weight[:, columns(my_tp)], preferred_element_type=F32
    )
    summed = hidden_in[:, columns(my_tp)].astype(F32) + own_part
    for step, copy in reversed(sum_copies):
        copy.wait_recv()
        summed = summed + sum_in[step].astype(F32)
    total[my_tp] = summed.astype(BF16)
    all_copies = []
    for step in (4, 3, 5, 2, 6, 1, 7):
        peer = lax.rem(my_tp + step, n_tp)
        copy = pltpu.make_async_remote_copy(
            src_ref=total.at[my_tp],
            dst_ref=total.at[my_tp],
            send_sem=all_send.at[step],
            recv_sem=all_recv.at[step],
            device_id={"tp": peer},
            device_id_type=MESH,
        )
        copy.start()
        all_copies.append(copy)
    for copy in reversed(all_copies):
        copy.wait_recv()
    blocks = [total[index].astype(F32) for index in range(n_tp)]
    square_sum = functools.reduce(jnp.add, [value * value for value in blocks])
    mean = jnp.sum(square_sum, axis=1, keepdims=True) / (block * n_tp)
    factor = lax.rsqrt(mean + 1e-05)
    for index, value in enumerate(blocks):
        cols = slice(index * block, (index + 1) * block)
        hidden_out[:, cols] = value.astype(BF16)
        normed_out[:, cols] = (value * factor * norm_gain[:, cols]).astype(BF16)
    for _, copy in sum_copies:
        copy.wait_send()
    for copy in all_copies:
        copy.wait_send()
    for slot in range(SLOTS):
        wait_bytes(outgoing.at[slot], mig_send.at[slot])
        wait_bytes(arrived.at[slot], mig_recv.at[slot])

    @pl.when(my_y == 1)
    def _():
        for slot in range(MIG_CAP):
            wait_bytes(arrived.at[SLOTS + slot], mig_send.at[SLOTS + slot])


def store_kernel(*refs):
    count = len(refs) // 2
    copies = [
        pltpu.make_async_copy(
            refs[index].at[pl.ds(start, step)],
            refs[count + index].at[pl.ds(start, step)],
            refs[-1].at[index],
        )
        for index in range(count)
        for step in [refs[count + index].shape[0] // (4 if index == count - 1 else 1)]
        for start in range(0, refs[count + index].shape[0], step)
    ]
    for copy in copies:
        copy.start()
    for copy in copies:
        copy.wait()


def shards(
    n_req,
    n_tp,
    hidden_in,
    query,
    new_kv,
    pool_cache,
    prompt_table,
    prompt_len,
    req_group,
    cont_table,
    cont_len,
    migration,
    diff_lambda,
    out_weight,
    norm_gain,
):
    rows, model = hidden_in.shape
    pages, page_len, width = pool_cache.shape
    span = cont_table.shape[1] * page_len
    block = model // n_tp
    operands = (
        prompt_table,
        prompt_len,
        req_group,
        cont_table.T,
        cont_len,
        migration.T,
        diff_lambda,
        hidden_in,
        query,
        new_kv,
        norm_gain.reshape(1, model),
        pool_cache,
        out_weight,
    )
    anywhere = pl.BlockSpec(memory_space=pl.ANY)
    vmem = pl.BlockSpec(memory_space=pltpu.VMEM)
    shapes = ((rows, model), (rows, model), (SLOTS, span, width))
    landing = ((rows, model), (rows, model), (SLOTS + RELAYS, span, width))
    results = pl.pallas_call(
        functools.partial(layer_kernel, n_req, n_tp),
        out_shape=tuple(pltpu.VMEM(shape, BF16) for shape in landing),
        in_specs=[anywhere] * len(operands),
        out_specs=(vmem,) * len(shapes),
        scratch_shapes=[
            *(pltpu.SMEM(value.shape, value.dtype) for value in operands[:7]),
            *(pltpu.VMEM(value.shape, value.dtype) for value in operands[7:]),
            pltpu.VMEM((rows, width), F32),
            pltpu.VMEM((rows, out_weight.shape[0]), BF16),
            pltpu.VMEM((SLOTS, span, width), BF16),
            pltpu.VMEM((n_tp, rows, block), BF16),
            pltpu.VMEM((n_tp, rows, block), BF16),
            pltpu.VMEM((n_tp, rows, block), BF16),
            pltpu.SemaphoreType.REGULAR((2,)),
            pltpu.SemaphoreType.DMA((11,)),
            pltpu.SemaphoreType.DMA((POOL_CHUNKS,)),
            pltpu.SemaphoreType.DMA,
            pltpu.SemaphoreType.DMA((SLOTS + RELAYS,)),
            pltpu.SemaphoreType.DMA((SLOTS + RELAYS * CONT_PAGES,)),
            pltpu.SemaphoreType.DMA((n_tp,)),
            pltpu.SemaphoreType.DMA((n_tp,)),
            pltpu.SemaphoreType.DMA((n_tp,)),
            pltpu.SemaphoreType.DMA((n_tp,)),
        ],
        compiler_params=pltpu.CompilerParams(collective_id=0, has_side_effects=True),
        name="decode_layer",
    )(*operands)
    return pl.pallas_call(
        store_kernel,
        out_shape=tuple(jax.ShapeDtypeStruct(shape, BF16) for shape in shapes),
        in_specs=[vmem] * len(shapes),
        out_specs=(anywhere,) * len(shapes),
        scratch_shapes=[pltpu.SemaphoreType.DMA((len(shapes),))],
        name="store_results",
    )(*(pltpu.with_memory_space_constraint(value, pltpu.VMEM) for value in results))


def solution(mesh):
    placed = (
        P("req", None),
        P("req", "tp"),
        P("req", "tp"),
        P("req", None, "tp"),
        P("req", None),
        P("req"),
        P("req"),
        P("req", None),
        P("req"),
        P("req", None),
        P("tp"),
        P("tp", None),
        P(),
    )
    return jax.shard_map(
        functools.partial(shards, mesh.shape["req"], mesh.shape["tp"]),
        mesh=mesh,
        in_specs=placed,
        out_specs=(P("req", None), P("req", None), P("req", None, "tp")),
        check_vma=False,
    )
```
